256 devices in a mesh: tm: 16 (over z_lo, x, core), space: 16 (over z_hi, y).
Axes of the slice: x: 4, y: 4, z: 8 (z_hi: 4, z_lo: 2; z = z_hi * 2 + z_lo), core: 2. Of those that a mesh axis runs over, the one named last changes fastest.
Arguments:
- tokens: bfloat16 [1680, 64, 256], P('space', 'tm'), may hold values from -11 to 11
- w_query: bfloat16 [256, 256], replicated, may hold values from -0.375 to 0.375
- w_key: bfloat16 [256, 256], replicated, may hold values from -0.375 to 0.375
- w_value: bfloat16 [256, 256], replicated, may hold values from -0.375 to 0.375
- w_out: bfloat16 [256, 256], replicated, may hold values from -0.375 to 0.375
- mask: int32 [1680, 1680], P('space'), may hold values from 0 to 1, as said below
- decay: float32 [64, 256], P('tm'), may hold values from 0 to 1
- cotangent: float32 [1680, 64, 256], P('space', 'tm'), may hold values from -6 to 6
Outputs:
- grad_tokens: float32 [1680, 64, 256], P('space', 'tm')
- grad_wq: float32 [256, 256], replicated
- grad_wk: float32 [256, 256], replicated
- grad_wv: float32 [256, 256], replicated
- output_weight_gradient: float32 [256, 256], replicated
The draws below stay inside these ranges and needn't reach their ends.
Inputs may be any that keep to these rules, and one draw needn't show every extreme that they name: `mask`: every token may attend to itself.
All inputs are finite; a program needn't handle non-finite values.
Results may differ from the reference program's by a relative error of at most 0.03.
The reference program's roundings to bfloat16 on the way count: a program that leaves them out, or rounds other values in their place, can miss the bound.
Values may be sent and summed in bfloat16 or wider, within the bound.
A program may use at most 128 MiB of HBM per device.

```python
import math
import jax
import jax.numpy as jnp
from jax import lax

D = 256
HEADS = 8
S = 1680
DECODE_SPAN = 64
N_SPACE = 16


def draw_tokens(key, part):
    first_key = jax.random.fold_in(key, 0)
    base = jnp.clip(jax.random.normal(first_key, (S, DECODE_SPAN, D)), -6.0, 6.0)
    return base.astype(jnp.bfloat16)


def draw_mask(key, part):
    levels = jax.random.randint(key, (S, S), 0, 4)
    diagonal = jnp.eye(S, dtype=jnp.int32)
    return jnp.maximum(jnp.minimum(levels, 1), diagonal).astype(jnp.int32)


def draw_decay(key, part):
    key_rate = jax.random.fold_in(key, 11)
    key_jitter = jax.random.fold_in(key, 12)
    episode_noise_seed = jax.random.fold_in(key, 13)
    key_factor = jax.random.fold_in(key, 14)
    exponent = jax.random.uniform(key_rate, (1, D), minval=-1.0, maxval=1.5)
    rates = jnp.exp(exponent * 2.302585)
    jitter = jax.random.uniform(key_jitter, (DECODE_SPAN, D), minval=0.5, maxval=2.0)
    decay = jnp.exp(-2.3 * rates * jitter / DECODE_SPAN)
    cycles_per_episode = jax.random.randint(episode_noise_seed, (3,), 0, DECODE_SPAN)
    faulty_qubit_positions = jnp.any(jnp.arange(DECODE_SPAN)[:, None] == cycles_per_episode[None, :], axis=1)
    factor = jax.random.uniform(key_factor, (DECODE_SPAN, D), minval=0.5, maxval=0.8)
    return jnp.where(faulty_qubit_positions[:, None], decay * factor, decay).astype(jnp.float32)


def block_levels(own_key, dims, cuts, low, top_value):
    level, own = 1.0, jax.random.fold_in(own_key, 6)
    for position, blocks in cuts:
        heights = jnp.exp(jax.random.uniform(jax.random.fold_in(own, position), (blocks,), jnp.float32, low / len(cuts), top_value / len(cuts)))
        level = level * jnp.repeat(heights, dims[position] // blocks).reshape([-1 if axis == position else 1 for axis in range(len(dims))])
    return level


def gaussian(own_key, extent, scale, limit, cuts=(), kind=jnp.bfloat16):
    factor_of = block_levels(own_key, extent, cuts, -0.22, 0.18) if cuts else 1.0
    entries = jax.random.normal(own_key, extent, jnp.float32) * scale * factor_of
    return jnp.minimum(jnp.maximum(entries, -limit), limit).astype(kind)


def setup_inputs(seed: int = 0) -> dict:
    splits = jax.random.split(jax.random.key(seed), 9)
    return {
        "tokens": draw_tokens(jax.random.fold_in(splits[8], 71), 0),
        "w_query": gaussian(splits[1], (D, D), D ** -0.5, 0.375),
        "w_key": gaussian(splits[2], (D, D), D ** -0.5, 0.375),
        "w_value": gaussian(splits[3], (D, D), D ** -0.5, 0.375),
        "w_out": gaussian(splits[4], (D, D), D ** -0.5, 0.375),
        "mask": draw_mask(jax.random.fold_in(splits[8], 71), 0),
        "decay": draw_decay(jax.random.fold_in(splits[8], 71), 0),
        "cotangent": gaussian(splits[7], (S, DECODE_SPAN, D), 1.0, 6.0, ((0, 16), (1, 16)), jnp.float32),
    }


def reference(tokens, w_query, w_key, w_value, w_out, mask, decay, cotangent):
    head_size = D // HEADS
    score_scale = 1.0 / math.sqrt(head_size)
    x_rounds = jnp.swapaxes(tokens, 0, 1)
    flat_rows = x_rounds.reshape(-1, D)

    def project(weight):
        result = jnp.dot(flat_rows, weight, preferred_element_type=jnp.float32)
        return result.astype(jnp.bfloat16).reshape(DECODE_SPAN, S, HEADS, head_size)
    queries = project(w_query)
    keys = project(w_key)
    values = project(w_value)
    allowed = mask > 0

    def probs_of(q_round, k_round):
        scores = jnp.einsum('ihe,jhe->hij', q_round.astype(jnp.float32), k_round.astype(jnp.float32)) * score_scale
        scores = jnp.where(allowed[None], scores, -1e+30)
        maxima = lax.optimization_barrier(jnp.max(scores, axis=2, keepdims=True))
        expons = jnp.exp(scores - maxima)
        return expons / lax.optimization_barrier(jnp.sum(expons, axis=2, keepdims=True))

    def forward(round_index):
        probs = probs_of(queries[round_index], keys[round_index])
        probs_b = probs.astype(jnp.bfloat16)
        stack_result_matrix = jnp.einsum('hij,jhe->ihe', probs_b.astype(jnp.float32), values[round_index].astype(jnp.float32))
        return stack_result_matrix.astype(jnp.bfloat16)
    attended = lax.map(forward, jnp.arange(DECODE_SPAN))
    decay_next = jnp.concatenate([decay[1:], jnp.zeros((1, D), jnp.float32)], axis=0)
    cot_rounds = jnp.swapaxes(cotangent, 0, 1)

    def backstep(carry, inputs):
        cot_round, decay_round = inputs
        value_now = cot_round + decay_round[None] * carry
        return (value_now, value_now)
    unused, grads = lax.scan(backstep, jnp.zeros((S, D), jnp.float32), (cot_rounds, decay_next), reverse=True)
    grads_flat = grads.astype(jnp.bfloat16).reshape(-1, D)
    attended_flat = attended.reshape(-1, D)
    output_weight_gradient = jnp.dot(attended_flat.T, grads_flat, preferred_element_type=jnp.float32)
    upstream = jnp.dot(grads_flat, w_out.T, preferred_element_type=jnp.float32)
    upstream = upstream.astype(jnp.bfloat16).reshape(DECODE_SPAN, S, HEADS, head_size)
    deltas = lax.optimization_barrier(jnp.sum(upstream.astype(jnp.float32) * attended.astype(jnp.float32), axis=3))
    group_count = N_SPACE
    group_rows = S // N_SPACE

    def backward(round_index):
        q_round = queries[round_index].astype(jnp.float32)
        k_round = keys[round_index].astype(jnp.float32)
        v_round = values[round_index].astype(jnp.float32)
        up_round = upstream[round_index].astype(jnp.float32)
        probs = probs_of(queries[round_index], keys[round_index])
        probs_b = probs.astype(jnp.bfloat16)
        slopes = jnp.einsum('ihe,jhe->hij', up_round, v_round)
        delta_round = jnp.swapaxes(deltas[round_index], 0, 1)[:, :, None]
        score_grads = (probs * (slopes - delta_round)).astype(jnp.bfloat16)
        grad_q = (jnp.einsum('hij,jhe->ihe', score_grads.astype(jnp.float32), k_round) * score_scale).astype(jnp.bfloat16)
        grouped_scores = score_grads.astype(jnp.float32).reshape(HEADS, group_count, group_rows, S)
        grouped_queries = q_round.reshape(group_count, group_rows, HEADS, head_size)
        key_parts = (jnp.einsum('hgij,gihe->gjhe', grouped_scores, grouped_queries) * score_scale).astype(jnp.bfloat16)
        grad_k = lax.optimization_barrier(jnp.sum(key_parts.astype(jnp.float32), axis=0)).astype(jnp.bfloat16)
        clustered_likelihoods = probs_b.astype(jnp.float32).reshape(HEADS, group_count, group_rows, S)
        clustered_upstream_cotangent = up_round.reshape(group_count, group_rows, HEADS, head_size)
        value_parts = jnp.einsum('hgij,gihe->gjhe', clustered_likelihoods, clustered_upstream_cotangent).astype(jnp.bfloat16)
        grad_v = lax.optimization_barrier(jnp.sum(value_parts.astype(jnp.float32), axis=0)).astype(jnp.bfloat16)
        return (grad_q, grad_k, grad_v)
    grad_q, grad_k, grad_v = lax.map(backward, jnp.arange(DECODE_SPAN))
    grad_q_flat = grad_q.reshape(-1, D)
    grad_k_flat = grad_k.reshape(-1, D)
    grad_v_flat = grad_v.reshape(-1, D)
    grad_rows = grads.reshape(-1, D)
    grad_rows = grad_rows + jnp.dot(grad_q_flat, w_query.T, preferred_element_type=jnp.float32)
    grad_rows = grad_rows + jnp.dot(grad_k_flat, w_key.T, preferred_element_type=jnp.float32)
    grad_rows = grad_rows + jnp.dot(grad_v_flat, w_value.T, preferred_element_type=jnp.float32)
    grad_tokens = jnp.swapaxes(grad_rows.reshape(DECODE_SPAN, S, D), 0, 1)
    grad_wq = jnp.dot(flat_rows.T, grad_q_flat, preferred_element_type=jnp.float32)
    grad_wk = jnp.dot(flat_rows.T, grad_k_flat, preferred_element_type=jnp.float32)
    grad_wv = jnp.dot(flat_rows.T, grad_v_flat, preferred_element_type=jnp.float32)
    return (grad_tokens, grad_wq, grad_wk, grad_wv, output_weight_gradient)
```

```python
import functools
import math

import jax
import jax.numpy as jnp
from jax import lax
from jax.experimental import pallas as pl
from jax.experimental.pallas import tpu as pltpu
from jax.sharding import PartitionSpec as P

HEADS = 8
NS = 16
NT = 16
NY = 4
MESH = pl.DeviceIdType.MESH
BF = jnp.bfloat16
F32 = jnp.float32
NEG = -1e30
MIB = 1 << 20

VM = pl.BlockSpec(memory_space=pltpu.VMEM)
ANY = pl.BlockSpec(memory_space=pl.ANY)


def params(mib=48, cid=None):
    if cid is None:
        return pltpu.CompilerParams(vmem_limit_bytes=mib * MIB)
    return pltpu.CompilerParams(
        vmem_limit_bytes=mib * MIB, collective_id=cid, has_side_effects=True
    )


def sds(shape, dtype):
    return jax.ShapeDtypeStruct(shape, dtype)


def nt(a, b):
    return lax.dot_general(a, b, (((1,), (1,)), ((), ())), preferred_element_type=F32)


def tn(a, b):
    return lax.dot_general(a, b, (((0,), (0,)), ((), ())), preferred_element_type=F32)


def nn(a, b):
    return jnp.dot(a, b, preferred_element_type=F32)


def mask_kernel(rows, pad, mask_ref, bias_ref):
    groups = NS
    bias_ref[...] = jnp.full(bias_ref.shape, NEG, BF)
    bias = jnp.where(mask_ref[...] > 0, 0.0, NEG).astype(F32)
    for group in range(groups):
        bias_ref[0:rows, group * pad : group * pad + rows] = bias[
            :, group * rows : (group + 1) * rows
        ].astype(BF)


def prep_kernel(x_ref, wq_ref, wk_ref, wv_ref, ct_ref, decay_ref, kv_ref, q_ref, m_ref, d_ref):
    rounds, _, width = x_ref.shape
    for r in range(rounds):
        x = x_ref[r]
        kv_ref[r, :, 0:width] = nn(x, wk_ref[...]).astype(BF)
        kv_ref[r, :, width : 2 * width] = nn(x, wv_ref[...]).astype(BF)
        q_ref[r] = nn(x, wq_ref[...]).astype(BF)
    level = ct_ref[rounds - 1]
    reach = decay_ref[rounds - 1 : rounds, :]
    for r in range(rounds - 2, -1, -1):
        level = ct_ref[r] + decay_ref[r + 1 : r + 2, :] * level
        reach = reach * decay_ref[r : r + 1, :]
    m_ref[...] = (decay_ref[0:1, :] * level).astype(BF)
    d_ref[...] = jnp.broadcast_to(reach, d_ref.shape)


def mid_kernel(ct_ref, decay_ref, m_ref, d_ref, wo_ref, grads_ref, u_ref):
    rounds = ct_ref.shape[0]
    me = lax.axis_index("tm")
    carried = jnp.zeros(ct_ref.shape[1:], F32)
    for k in range(NT - 1, 0, -1):
        inside = me + k < NT
        moved = m_ref[k - 1].astype(F32) + d_ref[k - 1, 0:1, :] * carried
        carried = jnp.where(inside, moved, 0.0)
    level = ct_ref[rounds - 1] + carried
    for r in range(rounds - 1, -1, -1):
        if r < rounds - 1:
            level = ct_ref[r] + decay_ref[r + 1 : r + 2, :] * level
        grads_ref[r] = level
        u_ref[r] = nt(level.astype(BF), wo_ref[...]).astype(BF)


def attention_kernel(
    scale, q_ref, u_ref, kv_ref, bias_ref, qa_ref, dkv_ref,
    kt_ref, vt_ref, qt_ref, ut_ref, s_ref, p_ref, pb_ref, t_ref, ds_ref, acc_q, acc_a, dkt, dvt,
    l_ref,
):
    rows, width = q_ref.shape
    keys = kv_ref.shape[0]
    size = width // HEADS
    kt_ref[...] = kv_ref[:, 0:width].T
    vt_ref[...] = kv_ref[:, width : 2 * width].T
    qt_ref[...] = q_ref[...].T
    ut_ref[...] = u_ref[...].T
    acc_q[...] = jnp.zeros_like(acc_q)
    acc_a[...] = jnp.zeros_like(acc_a)
    chunk = 16

    def head(h, carry):
        own = lax.broadcasted_iota(jnp.int32, (rows, width), 1) // size == h
        here = pl.ds(pl.multiple_of(h * size, size), size)
        qh = jnp.where(own, q_ref[...].astype(F32), 0.0).astype(BF)
        uf = jnp.where(own, u_ref[...].astype(F32), 0.0)
        uh = uf.astype(BF)
        s_ref[...] = nn(qh, kt_ref[...])

        def soft(i, c):
            at = pl.ds(pl.multiple_of(i * chunk, chunk), chunk)
            x = s_ref[at, :] * scale + bias_ref[at, :].astype(F32)
            e = jnp.exp(x - jnp.max(x, axis=1, keepdims=True))
            p = e * (1.0 / jnp.sum(e, axis=1, keepdims=True))
            p_ref[at, :] = p
            pb_ref[at, :] = p.astype(BF)
            return c

        lax.fori_loop(0, rows // chunk, soft, 0)
        a = nn(pb_ref[...], kv_ref[:, width : 2 * width]).astype(BF).astype(F32)
        acc_a[...] = jnp.where(own, a, acc_a[...])
        l_ref[...] = jnp.broadcast_to(jnp.sum(uf * a, axis=1, keepdims=True), l_ref.shape)
        t_ref[...] = nn(uh, vt_ref[...])

        def back(i, c):
            at = pl.ds(pl.multiple_of(i * chunk, chunk), chunk)
            ds_ref[at, :] = (p_ref[at, :] * (t_ref[at, :] - l_ref[at, 0:1])).astype(BF)
            return c

        lax.fori_loop(0, rows // chunk, back, 0)
        acc_q[...] = jnp.where(own, nn(ds_ref[...], kv_ref[:, 0:width]), acc_q[...])
        dkt[here, :] = nn(qt_ref[here, :], ds_ref[...])
        dvt[here, :] = nn(ut_ref[here, :], pb_ref[...])
        return carry

    lax.fori_loop(0, HEADS, head, 0)
    qa_ref[:, 0:width] = (acc_q[...] * scale).astype(BF)
    qa_ref[:, width : 2 * width] = acc_a[...].astype(BF)
    dkv_ref[:, 0:width] = (dkt[...] * scale).T.astype(BF)
    dkv_ref[:, width : 2 * width] = dvt[...].T.astype(BF)


def final_kernel(
    x_ref, grads_ref, qa_ref, part_ref, wq_ref, wk_ref, wv_ref, gt_ref, g_ref
):
    rounds, _, width = x_ref.shape
    half = width // 2
    gq = jnp.zeros((width, width), F32)
    gk, gv, go = gq, gq, gq
    for r in range(rounds):
        total = part_ref[r].astype(F32)
        for z in range(1, NS // NY):
            total = total + part_ref[z * NY + r].astype(F32)
        dk = total[:, 0:width].astype(BF)
        dv = total[:, width : 2 * width].astype(BF)
        dq = qa_ref[r, :, 0:width]
        att = qa_ref[r, :, width : 2 * width]
        grads = grads_ref[r]
        x = x_ref[r]
        gt_ref[r] = grads + nt(dq, wq_ref[...]) + nt(dk, wk_ref[...]) + nt(dv, wv_ref[...])
        gq += tn(x, dq)
        gk += tn(x, dk)
        gv += tn(x, dv)
        go += tn(att, grads.astype(BF))
    for i, g in enumerate((gq, gk, gv, go)):
        g_ref[2 * i] = g[:, 0:half]
        g_ref[2 * i + 1] = g[:, half:width]


def greet(axes):
    barrier = pltpu.get_barrier_semaphore()
    count = 0
    for axis, extent in axes:
        me = lax.axis_index(axis)
        for k in range(1, extent):
            pl.semaphore_signal(
                barrier, inc=1, device_id={axis: lax.rem(me + k, extent)}, device_id_type=MESH
            )
            count += 1
    pl.semaphore_wait(barrier, count)


def push(src, dst, sems, i, axis, to):
    return pltpu.make_async_remote_copy(
        src_ref=src,
        dst_ref=dst,
        send_sem=sems[0].at[i],
        recv_sem=sems[1].at[i],
        device_id={axis: to},
        device_id_type=MESH,
    )


def gather_kernel(
    kv_in, q_in, b_in, m_in, d_in, kv_out, q_out, b_out, m_out, d_out,
    s0, r0, s1, r1, s2, r2, s3, r3, s4, r4, own,
):
    me = lax.axis_index("space")
    y = lax.rem(me, NY)
    base = me - y
    t = lax.axis_index("tm")
    greet((("space", NS), ("tm", NT)))
    copies = []
    for k in range(1, NT):
        for src, dst, sems in ((m_in, m_out, (s3, r3)), (d_in, d_out, (s4, r4))):
            copy = push(src, dst.at[k - 1], sems, k, "tm", jnp.maximum(t - k, 0))
            pl.when(t >= k)(copy.start)
    for k in range(1, NY):
        to = lax.rem(y + k, NY)
        copies.append(push(q_in.at[to], q_out.at[y], (s1, r1), k, "space", base + to))
        copies.append(push(b_in, b_out.at[y], (s2, r2), k, "space", base + to))
    for k in (8, 4, 12, 5, 13, 7, 11, 6, 14, 9, 10, 3, 1, 2, 15):
        to = lax.rem(me + k, NS)
        copies.append(push(kv_in.at[lax.rem(to, NY)], kv_out.at[me], (s0, r0), k, "space", to))
    for copy in copies:
        copy.start()
    locals_ = [
        pltpu.make_async_copy(kv_in.at[y], kv_out.at[me], own.at[0]),
        pltpu.make_async_copy(q_in.at[y], q_out.at[y], own.at[1]),
        pltpu.make_async_copy(b_in, b_out.at[y], own.at[2]),
    ]
    for copy in locals_:
        copy.start()
    for copy in locals_:
        copy.wait()
    for k in range(1, NT):
        for src, dst, sems in ((m_in, m_out, (s3, r3)), (d_in, d_out, (s4, r4))):
            copy = push(src, dst.at[k - 1], sems, k, "tm", jnp.maximum(t - k, 0))
            pl.when(t >= k)(copy.wait_send)
            pl.when(t + k < NT)(copy.wait_recv)
    for copy in copies:
        copy.wait()


def row_kernel(u_in, u_out, s0, r0, own):
    me = lax.axis_index("space")
    y = lax.rem(me, NY)
    base = me - y
    barrier = pltpu.get_barrier_semaphore()
    for k in range(1, NY):
        pl.semaphore_signal(
            barrier, inc=1, device_id={"space": base + lax.rem(y + k, NY)}, device_id_type=MESH
        )
    pl.semaphore_wait(barrier, NY - 1)
    copies = []
    for k in range(1, NY):
        to = lax.rem(y + k, NY)
        copies.append(push(u_in.at[to], u_out.at[y], (s0, r0), k, "space", base + to))
    copies.append(pltpu.make_async_copy(u_in.at[y], u_out.at[y], own))
    for copy in copies:
        copy.start()
    for copy in copies:
        copy.wait()


def scatter_kernel(qa_in, part_in, qa_out, part_out, s0, r0, s1, r1, own):
    me = lax.axis_index("space")
    y = lax.rem(me, NY)
    base = me - y
    greet((("space", NS),))
    copies = []
    for k in (8, 4, 12, 5, 13, 7, 11, 6, 14, 9, 10, 3, 1, 2, 15):
        to = lax.rem(me + k, NS)
        copies.append(push(part_in.at[to], part_out.at[me], (s0, r0), k, "space", to))
    for k in range(1, NY):
        to = lax.rem(y + k, NY)
        copies.append(push(qa_in.at[to], qa_out.at[y], (s1, r1), k, "space", base + to))
    copies.append(pltpu.make_async_copy(part_in.at[me], part_out.at[me], own.at[0]))
    copies.append(pltpu.make_async_copy(qa_in.at[y], qa_out.at[y], own.at[1]))
    for copy in copies:
        copy.start()
    for copy in copies:
        copy.wait()


def reduce_kernel(
    g_in, g_out, send1, got1, part, got2, mine, whole, send4,
    s0, r0, s1, r1, s2, r2, s3, r3,
):
    me = lax.axis_index("space")
    t = lax.axis_index("tm")
    for i in range(NT):
        send1[i] = g_in[i].astype(send1.dtype)
    greet((("space", NS), ("tm", NT)))

    first = []
    for k in range(1, NT):
        to = lax.rem(t + k, NT)
        first.append(push(send1.at[to], got1.at[t], (s0, r0), k, "tm", to))
    for copy in first:
        copy.start()
    total = g_in[t]
    for copy in first:
        copy.wait()
    for k in range(1, NT):
        total = total + got1[lax.rem(t + k, NT)].astype(F32)
    part[...] = total.reshape(part.shape)

    second = []
    for k in range(1, NS):
        to = lax.rem(me + k, NS)
        second.append(push(part.at[to], got2.at[me], (s1, r1), k, "space", to))
    for copy in second:
        copy.start()
    total = part[me]
    for copy in second:
        copy.wait()
    for k in range(1, NS):
        total = total + got2[lax.rem(me + k, NS)]
    mine[...] = total
    whole[me] = total

    third = []
    for k in range(1, NS):
        to = lax.rem(me + k, NS)
        third.append(push(mine, whole.at[me], (s2, r2), k, "space", to))
    for copy in third:
        copy.start()
    for copy in third:
        copy.wait()
    send4[...] = whole[...].reshape(send4.shape).astype(send4.dtype)
    g_out[t] = send4[...]

    fourth = []
    for k in range(1, NT):
        to = lax.rem(t + k, NT)
        fourth.append(push(send4, g_out.at[t], (s3, r3), k, "tm", to))
    for copy in fourth:
        copy.start()
    for copy in fourth:
        copy.wait()


def dma(n):
    return pltpu.SemaphoreType.DMA((n,))


def shards(tokens, w_query, w_key, w_value, w_out, mask, decay, cotangent):
    rows, rounds, width = tokens.shape
    pad = -(-rows // 16) * 16
    keys = NS * pad
    quads = NY * pad
    scale = 1.0 / math.sqrt(width // HEADS)
    size = width // HEADS

    bias = pl.pallas_call(
        functools.partial(mask_kernel, rows, pad),
        out_shape=sds((pad, keys), BF),
        in_specs=[VM],
        out_specs=VM,
        compiler_params=params(),
        name="mask_rows",
    )(mask)
    widen = ((0, 0), (0, pad - rows), (0, 0))
    x = jnp.pad(jnp.swapaxes(tokens, 0, 1), widen)
    ct = jnp.pad(jnp.swapaxes(cotangent, 0, 1), widen)

    kv, q, update, reach = pl.pallas_call(
        prep_kernel,
        out_shape=(
            sds((rounds, pad, 2 * width), BF),
            sds((rounds, pad, width), BF),
            sds((pad, width), BF),
            sds((8, width), F32),
        ),
        in_specs=[VM] * 6,
        out_specs=[VM] * 4,
        compiler_params=params(),
        name="project",
    )(x, w_query, w_key, w_value, ct, decay)

    kv_all, q_all, bias_all, updates, reaches = pl.pallas_call(
        gather_kernel,
        out_shape=(
            sds((NS, pad, 2 * width), BF),
            sds((NY, pad, width), BF),
            sds((NY, pad, keys), BF),
            sds((NT - 1, pad, width), BF),
            sds((NT - 1, 8, width), F32),
        ),
        in_specs=[ANY] * 5,
        out_specs=[ANY] * 5,
        scratch_shapes=[
            dma(NS), dma(NS), dma(NY), dma(NY), dma(NY), dma(NY),
            dma(NT), dma(NT), dma(NT), dma(NT), dma(3),
        ],
        compiler_params=params(cid=1),
        name="gather",
    )(kv, q, bias, update, reach)

    grads, u = pl.pallas_call(
        mid_kernel,
        out_shape=(sds((rounds, pad, width), F32), sds((rounds, pad, width), BF)),
        in_specs=[VM] * 5,
        out_specs=[VM] * 2,
        compiler_params=params(),
        name="recur",
    )(ct, decay, updates, reaches, w_out)

    u_all = pl.pallas_call(
        row_kernel,
        out_shape=sds((NY, pad, width), BF),
        in_specs=[ANY],
        out_specs=ANY,
        scratch_shapes=[dma(NY), dma(NY), pltpu.SemaphoreType.DMA],
        compiler_params=params(cid=2),
        name="upstream_rows",
    )(u)

    qa, dkv = pl.pallas_call(
        functools.partial(attention_kernel, scale),
        out_shape=(sds((quads, 2 * width), BF), sds((keys, 2 * width), BF)),
        in_specs=[VM] * 4,
        out_specs=[VM] * 2,
        scratch_shapes=[
            pltpu.VMEM((width, keys), BF),
            pltpu.VMEM((width, keys), BF),
            pltpu.VMEM((width, quads), BF),
            pltpu.VMEM((width, quads), BF),
            pltpu.VMEM((quads, keys), F32),
            pltpu.VMEM((quads, keys), F32),
            pltpu.VMEM((quads, keys), BF),
            pltpu.VMEM((quads, keys), F32),
            pltpu.VMEM((quads, keys), BF),
            pltpu.VMEM((quads, width), F32),
            pltpu.VMEM((quads, width), F32),
            pltpu.VMEM((width, keys), F32),
            pltpu.VMEM((width, keys), F32),
            pltpu.VMEM((quads, 128), F32),
        ],
        compiler_params=params(56),
        name="attention",
    )(
        q_all.reshape(quads, width),
        u_all.reshape(quads, width),
        kv_all.reshape(keys, 2 * width),
        bias_all.reshape(quads, keys),
    )

    qa_own, parts = pl.pallas_call(
        scatter_kernel,
        out_shape=(sds((NY, pad, 2 * width), BF), sds((NS, pad, 2 * width), BF)),
        in_specs=[ANY] * 2,
        out_specs=[ANY] * 2,
        scratch_shapes=[dma(NS), dma(NS), dma(NY), dma(NY), dma(2)],
        compiler_params=params(cid=3),
        name="scatter",
    )(qa.reshape(NY, pad, 2 * width), dkv.reshape(NS, pad, 2 * width))

    gt, g = pl.pallas_call(
        final_kernel,
        out_shape=(sds((rounds, pad, width), F32), sds((8, width, 128), F32)),
        in_specs=[VM] * 7,
        out_specs=[VM] * 2,
        compiler_params=params(),
        name="finish",
    )(x, grads, qa_own, parts, w_query, w_key, w_value)

    wire = BF
    g = pl.pallas_call(
        reduce_kernel,
        out_shape=sds((NT, 128, 128), wire),
        in_specs=[VM],
        out_specs=VM,
        scratch_shapes=[
            pltpu.VMEM((NT, 128, 128), wire),
            pltpu.VMEM((NT, 128, 128), wire),
            pltpu.VMEM((NS, 8, 128), F32),
            pltpu.VMEM((NS, 8, 128), F32),
            pltpu.VMEM((8, 128), F32),
            pltpu.VMEM((NS, 8, 128), F32),
            pltpu.VMEM((128, 128), wire),
            dma(NT), dma(NT), dma(NS), dma(NS), dma(NS), dma(NS), dma(NT), dma(NT),
        ],
        compiler_params=params(cid=4),
        name="reduce_weights",
    )(g.reshape(NT, 128, 128))
    g = g.astype(F32).reshape(4, 2, width, 128)
    g = jnp.concatenate([g[:, 0], g[:, 1]], axis=2)
    grad_tokens = jnp.swapaxes(gt[:, :rows], 0, 1)
    return (grad_tokens, g[0], g[1], g[2], g[3])


def solution(mesh):
    return jax.shard_map(
        shards,
        mesh=mesh,
        in_specs=(
            P("space", "tm", None),
            P(),
            P(),
            P(),
            P(),
            P("space", None),
            P("tm", None),
            P("space", "tm", None),
        ),
        out_specs=(P("space", "tm", None), P(), P(), P(), P()),
        check_vma=False,
    )
```

```python
import functools
import math

import jax
import jax.numpy as jnp
from jax import lax
from jax.experimental import pallas as pl
from jax.experimental.pallas import tpu as pltpu
from jax.sharding import PartitionSpec as P

HEADS = 8
NS = 16
NT = 16
NY = 4
MESH = pl.DeviceIdType.MESH
BF = jnp.bfloat16
F32 = jnp.float32
NEG = -1e30
MIB = 1 << 20

VM = pl.BlockSpec(memory_space=pltpu.VMEM)
ANY = pl.BlockSpec(memory_space=pl.ANY)


def params(mib=48, cid=None):
    if cid is None:
        return pltpu.CompilerParams(vmem_limit_bytes=mib * MIB)
    return pltpu.CompilerParams(
        vmem_limit_bytes=mib * MIB, collective_id=cid, has_side_effects=True
    )


def sds(shape, dtype):
    return jax.ShapeDtypeStruct(shape, dtype)


def nt(a, b):
    return lax.dot_general(a, b, (((1,), (1,)), ((), ())), preferred_element_type=F32)


def tn(a, b):
    return lax.dot_general(a, b, (((0,), (0,)), ((), ())), preferred_element_type=F32)


def nn(a, b):
    return jnp.dot(a, b, preferred_element_type=F32)


def mask_kernel(rows, pad, mask_ref, bias_ref):
    bias_ref[...] = jnp.full(bias_ref.shape, NEG, BF)
    bias = jnp.where(mask_ref[...] > 0, 0.0, NEG).astype(F32)
    for group in range(NS):
        bias_ref[0:rows, group * pad : group * pad + rows] = bias[
            :, group * rows : (group + 1) * rows
        ].astype(BF)


def attention_kernel(
    scale, x_ref, gb_ref, bias_ref, wq_ref, wk_ref, wv_ref, wo_ref, c_ref, g_ref,
    k_ref, v_ref, kt_ref, vt_ref, qt_ref, u_ref, ut_ref, q32, u32,
    s_ref, p_ref, pb_ref, t_ref, ds_ref, acc_q, acc_a, dkt, dvt,
):
    rows, width = gb_ref.shape
    size = width // HEADS
    half = width // 2
    first = pl.multiple_of(lax.axis_index("space") // NY * rows, rows)
    x = x_ref[...]
    xq = x_ref[pl.ds(first, rows), :]
    k_ref[...] = nn(x, wk_ref[...]).astype(BF)
    v_ref[...] = nn(x, wv_ref[...]).astype(BF)
    kt_ref[...] = nt(wk_ref[...].T, x).astype(BF)
    vt_ref[...] = nt(wv_ref[...].T, x).astype(BF)
    q = nn(xq, wq_ref[...]).astype(BF)
    qt_ref[...] = nt(wq_ref[...].T, xq).astype(BF)
    u_ref[...] = nt(gb_ref[...], wo_ref[...]).astype(BF)
    ut_ref[...] = nt(wo_ref[...], gb_ref[...]).astype(BF)
    for h in range(HEADS):
        q32[h] = q[:, h * size : (h + 1) * size]
        u32[h] = u_ref[:, h * size : (h + 1) * size]
    acc_q[...] = jnp.zeros_like(acc_q)
    acc_a[...] = jnp.zeros_like(acc_a)
    block, step = rows // 2, 16
    blocks = rows // block

    def head(h, carry):
        here = pl.ds(pl.multiple_of(h * size, size), size)
        own = lax.broadcasted_iota(jnp.int32, (block, width), 1) // size == h

        def scores(b):
            at = pl.ds(b * block, block)
            s_ref[at] = nn(q32[h, at, :], kt_ref[here, :])

        def slopes(b):
            at = pl.ds(b * block, block)
            t_ref[at] = nn(u32[h, at, :], vt_ref[here, :])

        def softmax(b):
            for i in range(block // step):
                at = pl.ds(b * block + i * step, step)
                z = s_ref[at, :] * scale + bias_ref[at, :].astype(F32)
                e = jnp.exp(z - jnp.max(z, axis=1, keepdims=True))
                p = e * (1.0 / jnp.sum(e, axis=1, keepdims=True))
                p_ref[at, :] = p
                pb_ref[at, :] = p.astype(BF)

        def attend(b):
            at = pl.ds(b * block, block)
            a = nn(pb_ref[at], v_ref[...]).astype(BF).astype(F32)
            a = jnp.where(own, a, 0.0)
            acc_a[at] += a
            return jnp.sum(u_ref[at].astype(F32) * a, axis=1, keepdims=True)

        def score_grads(b, deltas):
            for i in range(block // step):
                at = pl.ds(b * block + i * step, step)
                ds_ref[at, :] = (
                    p_ref[at, :] * (t_ref[at, :] - deltas[i * step : (i + 1) * step])
                ).astype(BF)
            at = pl.ds(b * block, block)
            acc_q[at] += jnp.where(own, nn(ds_ref[at], k_ref[...]), 0.0)

        scores(0)
        deltas = None
        for b in range(blocks):
            if b + 1 < blocks:
                scores(b + 1)
            slopes(b)
            softmax(b)
            if b > 0:
                score_grads(b - 1, deltas)
            deltas = attend(b)
        score_grads(blocks - 1, deltas)
        dkt[here, :] = nn(qt_ref[here, :], ds_ref[...])
        dvt[here, :] = nn(ut_ref[here, :], pb_ref[...])
        return carry

    lax.fori_loop(0, HEADS, head, 0)
    dq = (acc_q[...] * scale).astype(BF)
    dk = (dkt[...] * scale).astype(BF)
    dv = dvt[...].astype(BF)
    c_ref[...] = (nn(wk_ref[...], dk) + nn(wv_ref[...], dv)).T.astype(BF)
    own_rows = pl.ds(first, rows)
    back = nt(dq, wq_ref[...])
    c_ref[own_rows, :] = (c_ref[own_rows, :].astype(F32) + back).astype(BF)
    weights = (
        tn(xq, dq),
        nn(dk, x).T,
        nn(dv, x).T,
        tn(acc_a[...].astype(BF), gb_ref[...]),
    )
    for i, g in enumerate(weights):
        g_ref[2 * i] = g[:, 0:half]
        g_ref[2 * i + 1] = g[:, half:width]


SPREAD = (8, 4, 12, 5, 13, 7, 11, 6, 14, 9, 10, 3, 1, 2, 15)


def greet(axes):
    barrier = pltpu.get_barrier_semaphore()
    count = 0
    for axis, extent in axes:
        me = lax.axis_index(axis)
        for k in range(1, extent):
            pl.semaphore_signal(
                barrier, inc=1, device_id={axis: lax.rem(me + k, extent)}, device_id_type=MESH
            )
            count += 1
    pl.semaphore_wait(barrier, count)


def push(src, dst, sems, i, axis, to):
    return pltpu.make_async_remote_copy(
        src_ref=src,
        dst_ref=dst,
        send_sem=sems[0].at[i],
        recv_sem=sems[1].at[i],
        device_id={axis: to},
        device_id_type=MESH,
    )


def gather_kernel(
    x_in, b_in, ct_ref, decay_ref, x_out, b_out, gb_out, grads_ref,
    m_send, d_send, m_got, d_got, gb_send, carried,
    s0, r0, s1, r1, s2, r2, s3, r3, s4, r4, s5, r5, own,
):
    rounds = ct_ref.shape[0]
    cols = b_in.shape[1] // 2
    me = lax.axis_index("space")
    y = lax.rem(me, NY)
    base = me - y
    t = lax.axis_index("tm")
    core = lax.rem(t, 2)
    half = pl.ds(pl.multiple_of(core * cols, cols), cols)

    level = ct_ref[rounds - 1]
    reach = decay_ref[rounds - 1 : rounds, :]
    for r in range(rounds - 2, -1, -1):
        level = ct_ref[r] + decay_ref[r + 1 : r + 2, :] * level
        reach = reach * decay_ref[r : r + 1, :]
    m_send[...] = (decay_ref[0:1, :] * level).astype(BF)
    d_send[...] = jnp.broadcast_to(reach, d_send.shape)

    greet((("tm", NT), ("space", NS)))
    for k in range(1, NT):
        to = jnp.maximum(t - k, 0)
        pl.when(t >= k)(push(m_send, m_got.at[k - 1], (s3, r3), k, "tm", to).start)
        pl.when(t >= k)(push(d_send, d_got.at[k - 1], (s4, r4), k, "tm", to).start)
    tokens = []
    for k in SPREAD:
        to = lax.rem(me + k, NS)
        tokens.append(push(x_in.at[lax.rem(to, NY)], x_out.at[me], (s0, r0), k, "space", to))
    masks = []
    for k in range(1, NY):
        to = lax.rem(y + k, NY)
        masks.append(
            push(b_in.at[:, half], b_out.at[y, :, half], (s2, r2), k, "space", base + to)
        )
    local = [
        pltpu.make_async_copy(x_in.at[y], x_out.at[me], own.at[0]),
        pltpu.make_async_copy(b_in, b_out.at[y], own.at[1]),
    ]
    for copy in masks + tokens + local:
        copy.start()

    for k in range(1, NT):
        to = jnp.maximum(t - k, 0)
        for src, dst, sems in ((m_send, m_got, (s3, r3)), (d_send, d_got, (s4, r4))):
            copy = push(src, dst.at[k - 1], sems, k, "tm", to)
            pl.when(t + k < NT)(copy.wait_recv)
    carried[...] = jnp.zeros(carried.shape, F32)
    for k in range(NT - 1, 0, -1):

        @pl.when(t + k < NT)
        def _():
            carried[...] = m_got[k - 1].astype(F32) + d_got[k - 1, 0:1, :] * carried[...]

    level = ct_ref[rounds - 1] + carried[...]
    for r in range(rounds - 1, -1, -1):
        if r < rounds - 1:
            level = ct_ref[r] + decay_ref[r + 1 : r + 2, :] * level
        grads_ref[r] = level
        gb_send[r] = level.astype(BF)
    ups = []
    for k in range(1, NY):
        to = lax.rem(y + k, NY)
        ups.append(push(gb_send.at[to], gb_out.at[y], (s1, r1), k, "space", base + to))
    ups.append(pltpu.make_async_copy(gb_send.at[y], gb_out.at[y], own.at[2]))
    for copy in ups:
        copy.start()

    shared = []
    for k in range(1, NY):
        masks[k - 1].wait()
        src = lax.rem(y - k + NY, NY)
        copy = push(
            b_out.at[src, :, half], b_out.at[src, :, half], (s5, r5), k, "tm", t + 1 - 2 * core
        )
        copy.start()
        shared.append(copy)
    for k in range(1, NT):
        to = jnp.maximum(t - k, 0)
        for src, dst, sems in ((m_send, m_got, (s3, r3)), (d_send, d_got, (s4, r4))):
            pl.when(t >= k)(push(src, dst.at[k - 1], sems, k, "tm", to).wait_send)
    for copy in tokens + local + ups + shared:
        copy.wait()


def scatter_kernel(
    c_in, g_in, c_out, g_out, send1, got1, part, got2, mine, whole, send4,
    s0, r0, s1, r1, s2, r2, s3, r3, s4, r4, own,
):
    me = lax.axis_index("space")
    t = lax.axis_index("tm")
    for i in range(NT):
        send1[i] = g_in[i].astype(send1.dtype)
    greet((("tm", NT), ("space", NS)))

    first = []
    for k in range(1, NT):
        to = lax.rem(t + k, NT)
        first.append(push(send1.at[to], got1.at[t], (s0, r0), k, "tm", to))
    tokens = []
    for k in SPREAD:
        to = lax.rem(me + k, NS)
        tokens.append(push(c_in.at[to], c_out.at[me], (s4, r4), k, "space", to))
    tokens.append(pltpu.make_async_copy(c_in.at[me], c_out.at[me], own))
    for copy in first + tokens:
        copy.start()
    total = g_in[t]
    for copy in first:
        copy.wait()
    for k in range(1, NT):
        total = total + got1[lax.rem(t + k, NT)].astype(F32)
    part[...] = total.reshape(part.shape)

    second = []
    for k in range(1, NS):
        to = lax.rem(me + k, NS)
        second.append(push(part.at[to], got2.at[me], (s1, r1), k, "space", to))
    for copy in second:
        copy.start()
    total = part[me]
    for copy in second:
        copy.wait()
    for k in range(1, NS):
        total = total + got2[lax.rem(me + k, NS)]
    mine[...] = total
    whole[me] = total

    third = []
    for k in range(1, NS):
        to = lax.rem(me + k, NS)
        third.append(push(mine, whole.at[me], (s2, r2), k, "space", to))
    for copy in third:
        copy.start()
    for copy in third:
        copy.wait()
    send4[...] = whole[...].reshape(send4.shape).astype(send4.dtype)
    g_out[t] = send4[...]

    fourth = []
    for k in range(1, NT):
        to = lax.rem(t + k, NT)
        fourth.append(push(send4, g_out.at[t], (s3, r3), k, "tm", to))
    for copy in fourth:
        copy.start()
    for copy in fourth + tokens:
        copy.wait()


def dma(n):
    return pltpu.SemaphoreType.DMA((n,))


def shards(tokens, w_query, w_key, w_value, w_out, mask, decay, cotangent):
    rows, rounds, width = tokens.shape
    pad = -(-rows // 16) * 16
    keys = NS * pad
    quads = NY * pad
    size = width // HEADS
    scale = 1.0 / math.sqrt(size)

    bias = pl.pallas_call(
        functools.partial(mask_kernel, rows, pad),
        out_shape=sds((pad, keys), BF),
        in_specs=[VM],
        out_specs=VM,
        compiler_params=params(),
        name="mask_rows",
    )(mask)
    widen = ((0, 0), (0, pad - rows), (0, 0))
    x = jnp.pad(jnp.swapaxes(tokens, 0, 1), widen)
    ct = jnp.pad(jnp.swapaxes(cotangent, 0, 1), widen)

    x_all, bias_all, gb_all, grads = pl.pallas_call(
        gather_kernel,
        out_shape=(
            sds((NS, pad, width), BF),
            sds((NY, pad, keys), BF),
            sds((NY, pad, width), BF),
            sds((rounds, pad, width), F32),
        ),
        in_specs=[ANY, ANY, VM, VM],
        out_specs=[ANY, ANY, ANY, VM],
        scratch_shapes=[
            pltpu.VMEM((pad, width), BF),
            pltpu.VMEM((8, width), F32),
            pltpu.VMEM((NT - 1, pad, width), BF),
            pltpu.VMEM((NT - 1, 8, width), F32),
            pltpu.VMEM((rounds, pad, width), BF),
            pltpu.VMEM((pad, width), F32),
            dma(NS), dma(NS), dma(NY), dma(NY), dma(NY), dma(NY),
            dma(NT), dma(NT), dma(NT), dma(NT), dma(NY), dma(NY), dma(3),
        ],
        compiler_params=params(cid=1),
        name="gather",
    )(x, bias, ct, decay)

    c, g = pl.pallas_call(
        functools.partial(attention_kernel, scale),
        out_shape=(sds((keys, width), BF), sds((8, width, width // 2), F32)),
        in_specs=[VM] * 7,
        out_specs=[VM] * 2,
        scratch_shapes=[
            pltpu.VMEM((keys, width), BF),
            pltpu.VMEM((keys, width), BF),
            pltpu.VMEM((width, keys), BF),
            pltpu.VMEM((width, keys), BF),
            pltpu.VMEM((width, quads), BF),
            pltpu.VMEM((quads, width), BF),
            pltpu.VMEM((width, quads), BF),
            pltpu.VMEM((HEADS, quads, size), BF),
            pltpu.VMEM((HEADS, quads, size), BF),
            pltpu.VMEM((quads, keys), F32),
            pltpu.VMEM((quads, keys), F32),
            pltpu.VMEM((quads, keys), BF),
            pltpu.VMEM((quads, keys), F32),
            pltpu.VMEM((quads, keys), BF),
            pltpu.VMEM((quads, width), F32),
            pltpu.VMEM((quads, width), F32),
            pltpu.VMEM((width, keys), F32),
            pltpu.VMEM((width, keys), F32),
        ],
        compiler_params=params(58),
        name="attention",
    )(
        x_all.reshape(keys, width),
        gb_all.reshape(quads, width),
        bias_all.reshape(quads, keys),
        w_query, w_key, w_value, w_out,
    )

    wire = BF
    parts, g = pl.pallas_call(
        scatter_kernel,
        out_shape=(sds((NS, pad, width), BF), sds((NT, 128, 128), wire)),
        in_specs=[ANY, VM],
        out_specs=[ANY, VM],
        scratch_shapes=[
            pltpu.VMEM((NT, 128, 128), wire),
            pltpu.VMEM((NT, 128, 128), wire),
            pltpu.VMEM((NS, 8, 128), F32),
            pltpu.VMEM((NS, 8, 128), F32),
            pltpu.VMEM((8, 128), F32),
            pltpu.VMEM((NS, 8, 128), F32),
            pltpu.VMEM((128, 128), wire),
            dma(NT), dma(NT), dma(NS), dma(NS), dma(NS), dma(NS), dma(NT), dma(NT),
            dma(NS), dma(NS), pltpu.SemaphoreType.DMA,
        ],
        compiler_params=params(cid=2),
        name="scatter",
    )(c.reshape(NS, pad, width), g.reshape(NT, 128, 128))
    parts = parts.reshape(NS // NY, rounds, pad, width)
    gt = grads + sum(parts[z].astype(F32) for z in range(NS // NY))
    g = g.astype(F32).reshape(4, 2, width, 128)
    g = jnp.concatenate([g[:, 0], g[:, 1]], axis=2)
    grad_tokens = jnp.swapaxes(gt[:, :rows], 0, 1)
    return (grad_tokens, g[0], g[1], g[2], g[3])


def solution(mesh):
    return jax.shard_map(
        shards,
        mesh=mesh,
        in_specs=(
            P("space", "tm", None),
            P(),
            P(),
            P(),
            P(),
            P("space", None),
            P("tm", None),
            P("space", "tm", None),
        ),
        out_specs=(P("space", "tm", None), P(), P(), P(), P()),
        check_vma=False,
    )
```

```python
import functools
import math

import jax
import jax.numpy as jnp
from jax import lax
from jax.experimental import pallas as pl
from jax.experimental.pallas import tpu as pltpu
from jax.sharding import PartitionSpec as P

HEADS = 8
NS = 16
NT = 16
NY = 4
NJ = 8
NZ = 8
MESH = pl.DeviceIdType.MESH
BF = jnp.bfloat16
F32 = jnp.float32
NEG = -1e30
MIB = 1 << 20

VM = pl.BlockSpec(memory_space=pltpu.VMEM)
ANY = pl.BlockSpec(memory_space=pl.ANY)


def params(mib=48, cid=None):
    if cid is None:
        return pltpu.CompilerParams(vmem_limit_bytes=mib * MIB)
    return pltpu.CompilerParams(
        vmem_limit_bytes=mib * MIB, collective_id=cid, has_side_effects=True
    )


def sds(shape, dtype):
    return jax.ShapeDtypeStruct(shape, dtype)


def nt(a, b):
    return lax.dot_general(a, b, (((1,), (1,)), ((), ())), preferred_element_type=F32)


def tn(a, b):
    return lax.dot_general(a, b, (((0,), (0,)), ((), ())), preferred_element_type=F32)


def nn(a, b):
    return jnp.dot(a, b, preferred_element_type=F32)


def mask_kernel(rows, pad, mask_ref, bias_ref):
    bias_ref[...] = jnp.full(bias_ref.shape, NEG, BF)
    bias = jnp.where(mask_ref[...] > 0, 0.0, NEG).astype(F32)
    for group in range(NS):
        bias_ref[0:rows, group * pad : group * pad + rows] = bias[
            :, group * rows : (group + 1) * rows
        ].astype(BF)


def attention_kernel(
    scale, x_ref, gb_ref, bias_ref, wq_ref, wk_ref, wv_ref, wo_ref, c_ref, g_ref,
    k_ref, v_ref, kt_ref, vt_ref, qt_ref, u_ref, ut_ref, q32, u32,
    s_ref, p_ref, pb_ref, t_ref, ds_ref, acc_q, acc_a, dkt, dvt,
):
    rows, width = gb_ref.shape
    size = width // HEADS
    half = width // 2
    first = pl.multiple_of(lax.axis_index("space") // NY * rows, rows)
    x = x_ref[...]
    xq = x_ref[pl.ds(first, rows), :]
    k_ref[...] = nn(x, wk_ref[...]).astype(BF)
    v_ref[...] = nn(x, wv_ref[...]).astype(BF)
    kt_ref[...] = nt(wk_ref[...].T, x).astype(BF)
    vt_ref[...] = nt(wv_ref[...].T, x).astype(BF)
    q = nn(xq, wq_ref[...]).astype(BF)
    qt_ref[...] = nt(wq_ref[...].T, xq).astype(BF)
    u_ref[...] = nt(gb_ref[...], wo_ref[...]).astype(BF)
    ut_ref[...] = nt(wo_ref[...], gb_ref[...]).astype(BF)
    for h in range(HEADS):
        q32[h] = q[:, h * size : (h + 1) * size]
        u32[h] = u_ref[:, h * size : (h + 1) * size]
    acc_q[...] = jnp.zeros_like(acc_q)
    acc_a[...] = jnp.zeros_like(acc_a)
    block, step = rows // 2, 16
    blocks = rows // block

    def head(h, carry):
        here = pl.ds(pl.multiple_of(h * size, size), size)
        own = lax.broadcasted_iota(jnp.int32, (block, width), 1) // size == h

        def scores(b):
            at = pl.ds(b * block, block)
            s_ref[at] = nn(q32[h, at, :], kt_ref[here, :])

        def slopes(b):
            at = pl.ds(b * block, block)
            t_ref[at] = nn(u32[h, at, :], vt_ref[here, :])

        def softmax(b):
            for i in range(block // step):
                at = pl.ds(b * block + i * step, step)
                z = s_ref[at, :] * scale + bias_ref[at, :].astype(F32)
                e = jnp.exp(z - jnp.max(z, axis=1, keepdims=True))
                p = e * (1.0 / jnp.sum(e, axis=1, keepdims=True))
                p_ref[at, :] = p
                pb_ref[at, :] = p.astype(BF)

        def attend(b):
            at = pl.ds(b * block, block)
            a = nn(pb_ref[at], v_ref[...]).astype(BF).astype(F32)
            a = jnp.where(own, a, 0.0)
            acc_a[at] += a
            return jnp.sum(u_ref[at].astype(F32) * a, axis=1, keepdims=True)

        def score_grads(b, deltas):
            for i in range(block // step):
                at = pl.ds(b * block + i * step, step)
                ds_ref[at, :] = (
                    p_ref[at, :] * (t_ref[at, :] - deltas[i * step : (i + 1) * step])
                ).astype(BF)
            at = pl.ds(b * block, block)
            acc_q[at] += jnp.where(own, nn(ds_ref[at], k_ref[...]), 0.0)

        scores(0)
        deltas = None
        for b in range(blocks):
            if b + 1 < blocks:
                scores(b + 1)
            slopes(b)
            softmax(b)
            if b > 0:
                score_grads(b - 1, deltas)
            deltas = attend(b)
        score_grads(blocks - 1, deltas)
        dkt[here, :] = nn(qt_ref[here, :], ds_ref[...])
        dvt[here, :] = nn(ut_ref[here, :], pb_ref[...])
        return carry

    lax.fori_loop(0, HEADS, head, 0)
    dq = (acc_q[...] * scale).astype(BF)
    dk = (dkt[...] * scale).astype(BF)
    dv = dvt[...].astype(BF)
    c_ref[...] = (nn(wk_ref[...], dk) + nn(wv_ref[...], dv)).T.astype(BF)
    own_rows = pl.ds(first, rows)
    back = nt(dq, wq_ref[...])
    c_ref[own_rows, :] = (c_ref[own_rows, :].astype(F32) + back).astype(BF)
    weights = (
        tn(xq, dq),
        nn(dk, x).T,
        nn(dv, x).T,
        tn(acc_a[...].astype(BF), gb_ref[...]),
    )
    for i, g in enumerate(weights):
        g_ref[2 * i] = g[:, 0:half]
        g_ref[2 * i + 1] = g[:, half:width]


SPREAD = (8, 4, 12, 5, 13, 7, 11, 6, 14, 9, 10, 3, 1, 2, 15)


def greet(diagonal):
    me = lax.axis_index("space")
    t = lax.axis_index("tm")
    j = lax.rem(t, NJ)
    peers = [{"space": lax.rem(me + k, NS)} for k in range(1, NS)]
    peers += [{"tm": t - j + lax.rem(j + k, NJ)} for k in range(1, NJ)]
    across = lax.rem(t + NJ, NT)
    peers.append({"tm": across})
    if diagonal:
        peers += [{"tm": across, "space": lax.rem(me + NY * k, NS)} for k in range(1, NS // NY)]
    barrier = pltpu.get_barrier_semaphore()
    for peer in peers:
        pl.semaphore_signal(barrier, inc=1, device_id=peer, device_id_type=MESH)
    pl.semaphore_wait(barrier, len(peers))


def push(src, dst, sems, i, **to):
    return pltpu.make_async_remote_copy(
        src_ref=src,
        dst_ref=dst,
        send_sem=sems[0].at[i],
        recv_sem=sems[1].at[i],
        device_id=to,
        device_id_type=MESH,
    )


def gather_kernel(
    x_in, b_in, ct_ref, decay_ref, x_out, b_out, gb_out, grads_ref,
    got, late, late_in, gb_send, carried, run, prod, before,
    s0, r0, s1, r1, s2, r2, s3, r3, s4, r4, s5, r5, own,
):
    rounds, pad, _ = ct_ref.shape
    cols = b_in.shape[1] // 2
    me = lax.axis_index("space")
    y = lax.rem(me, NY)
    base = me - y
    t = lax.axis_index("tm")
    core = lax.rem(t, 2)
    j = lax.rem(t, NJ)
    upper = t >= NJ
    half = pl.ds(pl.multiple_of(core * cols, cols), cols)

    level = ct_ref[rounds - 1]
    reach = decay_ref[rounds - 1 : rounds, :]
    for r in range(rounds - 2, -1, -1):
        level = ct_ref[r] + decay_ref[r + 1 : r + 2, :] * level
        reach = reach * decay_ref[r : r + 1, :]
    got[j, 0:pad, :] = (decay_ref[0:1, :] * level).astype(BF)
    d0 = reach.astype(BF).astype(F32)
    d1 = (reach - d0).astype(BF).astype(F32)
    d2 = reach - d0 - d1
    row = lax.broadcasted_iota(jnp.int32, (16, reach.shape[1]), 0)
    got[j, pad : pad + 16, :] = jnp.where(row == 0, d0, jnp.where(row == 1, d1, d2)).astype(BF)

    greet(False)
    scan = []
    for k in range(1, NJ):
        to = t - j + lax.rem(j + k, NJ)
        scan.append(push(got.at[j], got.at[j], (s3, r3), k, tm=to))
    tokens = []
    for k in SPREAD:
        to = lax.rem(me + k, NS)
        tokens.append(push(x_in.at[lax.rem(to, NY)], x_out.at[me], (s0, r0), k, space=to))
    masks = []
    for k in range(1, NY):
        to = base + lax.rem(y + k, NY)
        masks.append(push(b_in.at[:, half], b_out.at[y, :, half], (s2, r2), k, space=to))
    local = [
        pltpu.make_async_copy(x_in.at[y], x_out.at[me], own.at[0]),
        pltpu.make_async_copy(b_in, b_out.at[y], own.at[1]),
    ]
    for copy in scan + masks + tokens + local:
        copy.start()

    for copy in scan:
        copy.wait()
    run[...] = jnp.zeros(run.shape, F32)
    prod[...] = jnp.ones(prod.shape, F32)
    for i in range(NJ - 1, -1, -1):

        @pl.when(j == i)
        def _():
            carried[...] = run[...]
            before[...] = prod[...]

        tail = got[i, pad : pad + 16, :].astype(F32)
        step = tail[0:1] + tail[1:2] + tail[2:3]
        run[...] = got[i, 0:pad, :].astype(F32) + step * run[...]
        prod[...] = step * prod[...]
    late[...] = run[...].astype(BF)
    over = push(late, late_in, (s4, r4), 0, tm=lax.rem(t + NJ, NT))
    pl.when(upper)(over.start)

    @pl.when(jnp.logical_not(upper))
    def _():
        over.wait_recv()
        carried[...] += before[0:1, :] * late_in[...].astype(F32)

    level = ct_ref[rounds - 1] + carried[...]
    for r in range(rounds - 1, -1, -1):
        if r < rounds - 1:
            level = ct_ref[r] + decay_ref[r + 1 : r + 2, :] * level
        grads_ref[r] = level
        gb_send[r] = level.astype(BF)
    ups = []
    for k in range(1, NY):
        to = lax.rem(y + k, NY)
        ups.append(push(gb_send.at[to], gb_out.at[y], (s1, r1), k, space=base + to))
    ups.append(pltpu.make_async_copy(gb_send.at[y], gb_out.at[y], own.at[2]))
    for copy in ups:
        copy.start()

    shared = []
    for k in range(1, NY):
        masks[k - 1].wait()
        piece = b_out.at[lax.rem(y - k + NY, NY), :, half]
        copy = push(piece, piece, (s5, r5), k, tm=t + 1 - 2 * core)
        copy.start()
        shared.append(copy)
    pl.when(upper)(over.wait_send)
    for copy in tokens + local + ups + shared:
        copy.wait()


def scatter_kernel(
    c_in, g_in, c_out, g_out, send1, got1, part, got2, send3, got3, got4,
    s0, r0, s1, r1, s2, r2, s3, r3, s4, r4, s5, r5, own,
):
    me = lax.axis_index("space")
    t = lax.axis_index("tm")
    y = lax.rem(me, NY)
    base = me - y
    j = lax.rem(t, NJ)
    line = lax.div(me, NY) * 2 + lax.div(t, NJ)
    for i in range(NJ):
        send1[i] = g_in[i].astype(send1.dtype)
    greet(True)

    first = []
    for k in range(1, NJ):
        to = lax.rem(j + k, NJ)
        first.append(push(send1.at[to], got1.at[j], (s0, r0), k, tm=t - j + to))
    tokens = []
    for k in SPREAD:
        to = lax.rem(me + k, NS)
        tokens.append(push(c_in.at[to], c_out.at[me], (s4, r4), k, space=to))
    tokens.append(pltpu.make_async_copy(c_in.at[me], c_out.at[me], own))
    for copy in first + tokens:
        copy.start()
    total = g_in[j]
    for copy in first:
        copy.wait()
    for k in range(1, NJ):
        total = total + got1[lax.rem(j + k, NJ)].astype(F32)
    part[...] = total.reshape(part.shape)

    second = []
    for k in range(1, NY):
        to = lax.rem(y + k, NY)
        second.append(push(part.at[to], got2.at[y], (s1, r1), k, space=base + to))
    for copy in second:
        copy.start()
    total = part[y]
    for copy in second:
        copy.wait()
    for k in range(1, NY):
        total = total + got2[lax.rem(y + k, NY)]
    send3[...] = total.astype(send3.dtype)
    got3[line] = send3[...]

    third = []
    for k in range(1, NZ):
        to = lax.rem(line + k, NZ)
        third.append(
            push(
                send3, got3.at[line], (s2, r2), k,
                tm=lax.rem(to, 2) * NJ + j, space=lax.div(to, 2) * NY + y,
            )
        )
    for copy in third:
        copy.start()
    for copy in third:
        copy.wait()
    total = got3[0].astype(F32)
    for i in range(1, NZ):
        total = total + got3[i].astype(F32)
    got4[y] = total.astype(got4.dtype)

    fourth = []
    for k in range(1, NY):
        to = base + lax.rem(y + k, NY)
        fourth.append(push(got4.at[y], got4.at[y], (s3, r3), k, space=to))
    for copy in fourth:
        copy.start()
    for copy in fourth:
        copy.wait()
    g_out[j] = got4[...].reshape(g_out.shape[1:])

    fifth = []
    for k in range(1, NJ):
        to = t - j + lax.rem(j + k, NJ)
        fifth.append(push(g_out.at[j], g_out.at[j], (s5, r5), k, tm=to))
    for copy in fifth:
        copy.start()
    for copy in fifth + tokens:
        copy.wait()


def dma(n):
    return pltpu.SemaphoreType.DMA((n,))


def shards(tokens, w_query, w_key, w_value, w_out, mask, decay, cotangent):
    rows, rounds, width = tokens.shape
    pad = -(-rows // 16) * 16
    keys = NS * pad
    quads = NY * pad
    size = width // HEADS
    scale = 1.0 / math.sqrt(size)

    bias = pl.pallas_call(
        functools.partial(mask_kernel, rows, pad),
        out_shape=sds((pad, keys), BF),
        in_specs=[VM],
        out_specs=VM,
        compiler_params=params(),
        name="mask_rows",
    )(mask)
    widen = ((0, 0), (0, pad - rows), (0, 0))
    x = jnp.pad(jnp.swapaxes(tokens, 0, 1), widen)
    ct = jnp.pad(jnp.swapaxes(cotangent, 0, 1), widen)

    x_all, bias_all, gb_all, grads = pl.pallas_call(
        gather_kernel,
        out_shape=(
            sds((NS, pad, width), BF),
            sds((NY, pad, keys), BF),
            sds((NY, pad, width), BF),
            sds((rounds, pad, width), F32),
        ),
        in_specs=[ANY, ANY, VM, VM],
        out_specs=[ANY, ANY, ANY, VM],
        scratch_shapes=[
            pltpu.VMEM((NJ, pad + 16, width), BF),
            pltpu.VMEM((pad, width), BF),
            pltpu.VMEM((pad, width), BF),
            pltpu.VMEM((rounds, pad, width), BF),
            pltpu.VMEM((pad, width), F32),
            pltpu.VMEM((pad, width), F32),
            pltpu.VMEM((8, width), F32),
            pltpu.VMEM((8, width), F32),
            dma(NS), dma(NS), dma(NY), dma(NY), dma(NY), dma(NY),
            dma(NJ), dma(NJ), dma(1), dma(1), dma(NY), dma(NY), dma(3),
        ],
        compiler_params=params(cid=1),
        name="gather",
    )(x, bias, ct, decay)

    c, g = pl.pallas_call(
        functools.partial(attention_kernel, scale),
        out_shape=(sds((keys, width), BF), sds((8, width, width // 2), F32)),
        in_specs=[VM] * 7,
        out_specs=[VM] * 2,
        scratch_shapes=[
            pltpu.VMEM((keys, width), BF),
            pltpu.VMEM((keys, width), BF),
            pltpu.VMEM((width, keys), BF),
            pltpu.VMEM((width, keys), BF),
            pltpu.VMEM((width, quads), BF),
            pltpu.VMEM((quads, width), BF),
            pltpu.VMEM((width, quads), BF),
            pltpu.VMEM((HEADS, quads, size), BF),
            pltpu.VMEM((HEADS, quads, size), BF),
            pltpu.VMEM((quads, keys), F32),
            pltpu.VMEM((quads, keys), F32),
            pltpu.VMEM((quads, keys), BF),
            pltpu.VMEM((quads, keys), F32),
            pltpu.VMEM((quads, keys), BF),
            pltpu.VMEM((quads, width), F32),
            pltpu.VMEM((quads, width), F32),
            pltpu.VMEM((width, keys), F32),
            pltpu.VMEM((width, keys), F32),
        ],
        compiler_params=params(58),
        name="attention",
    )(
        x_all.reshape(keys, width),
        gb_all.reshape(quads, width),
        bias_all.reshape(quads, keys),
        w_query, w_key, w_value, w_out,
    )

    wire = BF
    parts, g = pl.pallas_call(
        scatter_kernel,
        out_shape=(sds((NS, pad, width), BF), sds((NJ, 256, 128), wire)),
        in_specs=[ANY, VM],
        out_specs=[ANY, VM],
        scratch_shapes=[
            pltpu.VMEM((NJ, 256, 128), wire),
            pltpu.VMEM((NJ, 256, 128), wire),
            pltpu.VMEM((NY, 64, 128), F32),
            pltpu.VMEM((NY, 64, 128), F32),
            pltpu.VMEM((64, 128), wire),
            pltpu.VMEM((NZ, 64, 128), wire),
            pltpu.VMEM((NY, 64, 128), wire),
            dma(NJ), dma(NJ), dma(NY), dma(NY), dma(NZ), dma(NZ), dma(NY), dma(NY),
            dma(NS), dma(NS), dma(NJ), dma(NJ), pltpu.SemaphoreType.DMA,
        ],
        compiler_params=params(cid=2),
        name="scatter",
    )(c.reshape(NS, pad, width), g)
    parts = parts.reshape(NS // NY, rounds, pad, width)
    gt = grads + sum(parts[z].astype(F32) for z in range(NS // NY))
    g = g.astype(F32).reshape(4, 2, width, 128)
    g = jnp.concatenate([g[:, 0], g[:, 1]], axis=2)
    grad_tokens = jnp.swapaxes(gt[:, :rows], 0, 1)
    return (grad_tokens, g[0], g[1], g[2], g[3])


def solution(mesh):
    return jax.shard_map(
        shards,
        mesh=mesh,
        in_specs=(
            P("space", "tm", None),
            P(),
            P(),
            P(),
            P(),
            P("space", None),
            P("tm", None),
            P("space", "tm", None),
        ),
        out_specs=(P("space", "tm", None), P(), P(), P(), P()),
        check_vma=False,
    )
```

```python
import functools
import math

import jax
import jax.numpy as jnp
from jax import lax
from jax.experimental import pallas as pl
from jax.experimental.pallas import tpu as pltpu
from jax.sharding import PartitionSpec as P

HEADS = 8
NS = 16
NT = 16
NY = 4
NJ = 8
NZ = 8
MESH = pl.DeviceIdType.MESH
BF = jnp.bfloat16
F32 = jnp.float32
NEG = -1e30
MIB = 1 << 20

VM = pl.BlockSpec(memory_space=pltpu.VMEM)
ANY = pl.BlockSpec(memory_space=pl.ANY)


def params(mib=16, cid=None):
    if cid is None:
        return pltpu.CompilerParams(vmem_limit_bytes=mib * MIB)
    return pltpu.CompilerParams(
        vmem_limit_bytes=mib * MIB, collective_id=cid, has_side_effects=True
    )


def sds(shape, dtype):
    return jax.ShapeDtypeStruct(shape, dtype)


def nt(a, b):
    return lax.dot_general(a, b, (((1,), (1,)), ((), ())), preferred_element_type=F32)


def tn(a, b):
    return lax.dot_general(a, b, (((0,), (0,)), ((), ())), preferred_element_type=F32)


def nn(a, b):
    return jnp.dot(a, b, preferred_element_type=F32)


def mask_kernel(rows, pad, mask_ref, bias_ref):
    bias_ref[...] = jnp.full(bias_ref.shape, NEG, BF)
    bias = jnp.where(mask_ref[...] > 0, 0.0, NEG).astype(F32)
    for group in range(NS):
        bias_ref[0:rows, group * pad : group * pad + rows] = bias[
            :, group * rows : (group + 1) * rows
        ].astype(BF)


def attention_kernel(
    scale, x_ref, gb_ref, bias_ref, wq_ref, wk_ref, wv_ref, wo_ref, c_ref, g_ref,
    k_ref, v_ref, kt_ref, vt_ref, qt_ref, u_ref, ut_ref, q32, u32,
    s_ref, p_ref, pb_ref, t_ref, ds_ref, acc_q, acc_a, dkt, dvt,
):
    rows, width = gb_ref.shape
    size = width // HEADS
    half = width // 2
    first = pl.multiple_of(lax.axis_index("space") // NY * rows, rows)
    x = x_ref[...]
    xq = x_ref[pl.ds(first, rows), :]
    k_ref[...] = nn(x, wk_ref[...]).astype(BF)
    v_ref[...] = nn(x, wv_ref[...]).astype(BF)
    kt_ref[...] = nt(wk_ref[...].T, x).astype(BF)
    vt_ref[...] = nt(wv_ref[...].T, x).astype(BF)
    q = nn(xq, wq_ref[...]).astype(BF)
    qt_ref[...] = nt(wq_ref[...].T, xq).astype(BF)
    u_ref[...] = nt(gb_ref[...], wo_ref[...]).astype(BF)
    ut_ref[...] = nt(wo_ref[...], gb_ref[...]).astype(BF)
    for h in range(HEADS):
        q32[h] = q[:, h * size : (h + 1) * size]
        u32[h] = u_ref[:, h * size : (h + 1) * size]
    acc_q[...] = jnp.zeros_like(acc_q)
    acc_a[...] = jnp.zeros_like(acc_a)
    block, step = rows // 2, 16
    blocks = rows // block

    def head(h, carry):
        here = pl.ds(pl.multiple_of(h * size, size), size)
        own = lax.broadcasted_iota(jnp.int32, (block, width), 1) // size == h

        def scores(b):
            at = pl.ds(b * block, block)
            s_ref[at] = nn(q32[h, at, :], kt_ref[here, :])

        def slopes(b):
            at = pl.ds(b * block, block)
            t_ref[at] = nn(u32[h, at, :], vt_ref[here, :])

        def softmax(b):
            for i in range(block // step):
                at = pl.ds(b * block + i * step, step)
                z = s_ref[at, :] * scale + bias_ref[at, :].astype(F32)
                e = jnp.exp(z - jnp.max(z, axis=1, keepdims=True))
                p = e * (1.0 / jnp.sum(e, axis=1, keepdims=True))
                p_ref[at, :] = p
                pb_ref[at, :] = p.astype(BF)

        def attend(b):
            at = pl.ds(b * block, block)
            a = nn(pb_ref[at], v_ref[...]).astype(BF).astype(F32)
            a = jnp.where(own, a, 0.0)
            acc_a[at] += a
            return jnp.sum(u_ref[at].astype(F32) * a, axis=1, keepdims=True)

        def score_grads(b, deltas):
            for i in range(block // step):
                at = pl.ds(b * block + i * step, step)
                ds_ref[at, :] = (
                    p_ref[at, :] * (t_ref[at, :] - deltas[i * step : (i + 1) * step])
                ).astype(BF)
            at = pl.ds(b * block, block)
            acc_q[at] += jnp.where(own, nn(ds_ref[at], k_ref[...]), 0.0)

        scores(0)
        deltas = None
        for b in range(blocks):
            if b + 1 < blocks:
                scores(b + 1)
            slopes(b)
            softmax(b)
            if b > 0:
                score_grads(b - 1, deltas)
            deltas = attend(b)
        score_grads(blocks - 1, deltas)
        dkt[here, :] = nn(qt_ref[here, :], ds_ref[...])
        dvt[here, :] = nn(ut_ref[here, :], pb_ref[...])
        return carry

    lax.fori_loop(0, HEADS, head, 0)
    dq = (acc_q[...] * scale).astype(BF)
    dk = (dkt[...] * scale).astype(BF)
    dv = dvt[...].astype(BF)
    c_ref[...] = (nn(wk_ref[...], dk) + nn(wv_ref[...], dv)).T.astype(BF)
    own_rows = pl.ds(first, rows)
    back = nt(dq, wq_ref[...])
    c_ref[own_rows, :] = (c_ref[own_rows, :].astype(F32) + back).astype(BF)
    weights = (
        tn(xq, dq),
        nn(dk, x).T,
        nn(dv, x).T,
        tn(acc_a[...].astype(BF), gb_ref[...]),
    )
    for i, g in enumerate(weights):
        g_ref[2 * i] = g[:, 0:half]
        g_ref[2 * i + 1] = g[:, half:width]


SPREAD = (8, 4, 12, 5, 11, 9, 1, 13, 7, 6, 10, 14, 3, 2, 15)


def greet(diagonal):
    me = lax.axis_index("space")
    t = lax.axis_index("tm")
    j = lax.rem(t, NJ)
    peers = [{"space": lax.rem(me + k, NS)} for k in range(1, NS)]
    peers += [{"tm": t - j + lax.rem(j + k, NJ)} for k in range(1, NJ)]
    across = lax.rem(t + NJ, NT)
    peers.append({"tm": across})
    if diagonal:
        peers += [{"tm": across, "space": lax.rem(me + NY * k, NS)} for k in range(1, NS // NY)]
    barrier = pltpu.get_barrier_semaphore()
    for peer in peers:
        pl.semaphore_signal(barrier, inc=1, device_id=peer, device_id_type=MESH)
    return lambda: pl.semaphore_wait(barrier, len(peers))


def push(src, dst, sems, i, **to):
    return pltpu.make_async_remote_copy(
        src_ref=src,
        dst_ref=dst,
        send_sem=sems[0].at[i],
        recv_sem=sems[1].at[i],
        device_id=to,
        device_id_type=MESH,
    )


def gather_kernel(
    x_in, b_in, ct_ref, decay_ref, x_out, b_out, gb_out, grads_ref,
    got, late, late_in, gb_send, carried, run, prod, before,
    s0, r0, s1, r1, s2, r2, s3, r3, s4, r4, s5, r5, own,
):
    rounds, pad, _ = ct_ref.shape
    cols = b_in.shape[1] // 2
    me = lax.axis_index("space")
    y = lax.rem(me, NY)
    base = me - y
    t = lax.axis_index("tm")
    core = lax.rem(t, 2)
    j = lax.rem(t, NJ)
    upper = t >= NJ
    half = pl.ds(pl.multiple_of(core * cols, cols), cols)
    all_here = greet(False)

    level = ct_ref[rounds - 1]
    reach = decay_ref[rounds - 1 : rounds, :]
    for r in range(rounds - 2, -1, -1):
        level = ct_ref[r] + decay_ref[r + 1 : r + 2, :] * level
        reach = reach * decay_ref[r : r + 1, :]
    got[j, 0:pad, :] = (decay_ref[0:1, :] * level).astype(BF)
    d0 = reach.astype(BF).astype(F32)
    d1 = (reach - d0).astype(BF).astype(F32)
    d2 = reach - d0 - d1
    row = lax.broadcasted_iota(jnp.int32, (16, reach.shape[1]), 0)
    got[j, pad : pad + 16, :] = jnp.where(row == 0, d0, jnp.where(row == 1, d1, d2)).astype(BF)

    all_here()
    scan = []
    for k in range(1, NJ):
        to = t - j + lax.rem(j + k, NJ)
        scan.append(push(got.at[j], got.at[j], (s3, r3), k, tm=to))
    tokens = []
    for k in SPREAD:
        to = lax.rem(me + k, NS)
        tokens.append(push(x_in.at[lax.rem(to, NY)], x_out.at[me], (s0, r0), k, space=to))
    masks = []
    for k in range(1, NY):
        to = base + lax.rem(y + k, NY)
        masks.append(push(b_in.at[:, half], b_out.at[y, :, half], (s2, r2), k, space=to))
    local = [
        pltpu.make_async_copy(x_in.at[y], x_out.at[me], own.at[0]),
        pltpu.make_async_copy(b_in, b_out.at[y], own.at[1]),
    ]
    for copy in scan + masks + tokens + local:
        copy.start()

    for copy in scan:
        copy.wait()
    run[...] = jnp.zeros(run.shape, F32)
    prod[...] = jnp.ones(prod.shape, F32)
    for i in range(NJ - 1, -1, -1):

        @pl.when(j == i)
        def _():
            carried[...] = run[...]
            before[...] = prod[...]

        tail = got[i, pad : pad + 16, :].astype(F32)
        step = tail[0:1] + tail[1:2] + tail[2:3]
        run[...] = got[i, 0:pad, :].astype(F32) + step * run[...]
        prod[...] = step * prod[...]
    late[...] = run[...].astype(BF)
    over = push(late, late_in, (s4, r4), 0, tm=lax.rem(t + NJ, NT))
    pl.when(upper)(over.start)

    @pl.when(jnp.logical_not(upper))
    def _():
        over.wait_recv()
        carried[...] += before[0:1, :] * late_in[...].astype(F32)

    level = ct_ref[rounds - 1] + carried[...]
    for r in range(rounds - 1, -1, -1):
        if r < rounds - 1:
            level = ct_ref[r] + decay_ref[r + 1 : r + 2, :] * level
        grads_ref[r] = level
        gb_send[r] = level.astype(BF)
    ups = []
    for k in range(1, NY):
        to = lax.rem(y + k, NY)
        ups.append(push(gb_send.at[to], gb_out.at[y], (s1, r1), k, space=base + to))
    ups.append(pltpu.make_async_copy(gb_send.at[y], gb_out.at[y], own.at[2]))
    for copy in ups:
        copy.start()

    shared = []
    for k in range(1, NY):
        masks[k - 1].wait()
        piece = b_out.at[lax.rem(y - k + NY, NY), :, half]
        copy = push(piece, piece, (s5, r5), k, tm=t + 1 - 2 * core)
        copy.start()
        shared.append(copy)
    pl.when(upper)(over.wait_send)
    for copy in tokens + local + ups + shared:
        copy.wait()


def scatter_kernel(
    c_in, g_in, c_out, g_out, send1, got1, part, got2, send3, got3, got4,
    s0, r0, s1, r1, s2, r2, s3, r3, s4, r4, s5, r5, own,
):
    me = lax.axis_index("space")
    t = lax.axis_index("tm")
    y = lax.rem(me, NY)
    base = me - y
    j = lax.rem(t, NJ)
    line = lax.div(me, NY) * 2 + lax.div(t, NJ)
    all_here = greet(True)
    for i in range(NJ):
        send1[i] = g_in[i].astype(send1.dtype)
    all_here()

    first = []
    for k in range(1, NJ):
        to = lax.rem(j + k, NJ)
        first.append(push(send1.at[to], got1.at[j], (s0, r0), k, tm=t - j + to))
    tokens = []
    for k in SPREAD:
        to = lax.rem(me + k, NS)
        tokens.append(push(c_in.at[to], c_out.at[me], (s4, r4), k, space=to))
    tokens.append(pltpu.make_async_copy(c_in.at[me], c_out.at[me], own))
    early, later = tokens[:7] + tokens[-1:], tokens[7:-1]
    for copy in first + early:
        copy.start()
    total = g_in[j]
    for copy in first:
        copy.wait()
    for k in range(1, NJ):
        total = total + got1[lax.rem(j + k, NJ)].astype(F32)
    part[...] = total.reshape(part.shape)

    second = []
    for k in range(1, NY):
        to = lax.rem(y + k, NY)
        second.append(push(part.at[to], got2.at[y], (s1, r1), k, space=base + to))
    for copy in second:
        copy.start()
    total = part[y]
    for copy in second:
        copy.wait()
    for k in range(1, NY):
        total = total + got2[lax.rem(y + k, NY)]
    send3[...] = total.astype(send3.dtype)
    got3[line] = send3[...]

    third = []
    for k in range(1, NZ):
        to = lax.rem(line + k, NZ)
        third.append(
            push(
                send3, got3.at[line], (s2, r2), k,
                tm=lax.rem(to, 2) * NJ + j, space=lax.div(to, 2) * NY + y,
            )
        )
    for copy in third + later:
        copy.start()
    for copy in third:
        copy.wait()
    total = got3[0].astype(F32)
    for i in range(1, NZ):
        total = total + got3[i].astype(F32)
    got4[y] = total.astype(got4.dtype)

    fourth = []
    for k in range(1, NY):
        to = base + lax.rem(y + k, NY)
        fourth.append(push(got4.at[y], got4.at[y], (s3, r3), k, space=to))
    for copy in fourth:
        copy.start()
    for copy in fourth:
        copy.wait()
    g_out[j] = got4[...].reshape(g_out.shape[1:])

    fifth = []
    for k in range(1, NJ):
        to = t - j + lax.rem(j + k, NJ)
        fifth.append(push(g_out.at[j], g_out.at[j], (s5, r5), k, tm=to))
    for copy in fifth:
        copy.start()
    for copy in fifth + tokens:
        copy.wait()


def dma(n):
    return pltpu.SemaphoreType.DMA((n,))


def shards(tokens, w_query, w_key, w_value, w_out, mask, decay, cotangent):
    rows, rounds, width = tokens.shape
    pad = -(-rows // 16) * 16
    keys = NS * pad
    quads = NY * pad
    size = width // HEADS
    scale = 1.0 / math.sqrt(size)

    bias = pl.pallas_call(
        functools.partial(mask_kernel, rows, pad),
        out_shape=sds((pad, keys), BF),
        in_specs=[VM],
        out_specs=VM,
        compiler_params=params(),
        name="mask_rows",
    )(mask)
    widen = ((0, 0), (0, pad - rows), (0, 0))
    x = jnp.pad(jnp.swapaxes(tokens, 0, 1), widen)
    ct = jnp.pad(jnp.swapaxes(cotangent, 0, 1), widen)

    x_all, bias_all, gb_all, grads = pl.pallas_call(
        gather_kernel,
        out_shape=(
            sds((NS, pad, width), BF),
            sds((NY, pad, keys), BF),
            sds((NY, pad, width), BF),
            sds((rounds, pad, width), F32),
        ),
        in_specs=[ANY, ANY, VM, VM],
        out_specs=[ANY, ANY, ANY, VM],
        scratch_shapes=[
            pltpu.VMEM((NJ, pad + 16, width), BF),
            pltpu.VMEM((pad, width), BF),
            pltpu.VMEM((pad, width), BF),
            pltpu.VMEM((rounds, pad, width), BF),
            pltpu.VMEM((pad, width), F32),
            pltpu.VMEM((pad, width), F32),
            pltpu.VMEM((8, width), F32),
            pltpu.VMEM((8, width), F32),
            dma(NS), dma(NS), dma(NY), dma(NY), dma(NY), dma(NY),
            dma(NJ), dma(NJ), dma(1), dma(1), dma(NY), dma(NY), dma(3),
        ],
        compiler_params=params(cid=1),
        name="gather",
    )(x, bias, ct, decay)

    c, g = pl.pallas_call(
        functools.partial(attention_kernel, scale),
        out_shape=(sds((keys, width), BF), sds((8, width, width // 2), F32)),
        in_specs=[VM] * 7,
        out_specs=[VM] * 2,
        scratch_shapes=[
            pltpu.VMEM((keys, width), BF),
            pltpu.VMEM((keys, width), BF),
            pltpu.VMEM((width, keys), BF),
            pltpu.VMEM((width, keys), BF),
            pltpu.VMEM((width, quads), BF),
            pltpu.VMEM((quads, width), BF),
            pltpu.VMEM((width, quads), BF),
            pltpu.VMEM((HEADS, quads, size), BF),
            pltpu.VMEM((HEADS, quads, size), BF),
            pltpu.VMEM((quads, keys), F32),
            pltpu.VMEM((quads, keys), F32),
            pltpu.VMEM((quads, keys), BF),
            pltpu.VMEM((quads, keys), F32),
            pltpu.VMEM((quads, keys), BF),
            pltpu.VMEM((quads, width), F32),
            pltpu.VMEM((quads, width), F32),
            pltpu.VMEM((width, keys), F32),
            pltpu.VMEM((width, keys), F32),
        ],
        compiler_params=params(42),
        name="attention",
    )(
        x_all.reshape(keys, width),
        gb_all.reshape(quads, width),
        bias_all.reshape(quads, keys),
        w_query, w_key, w_value, w_out,
    )

    wire = BF
    parts, g = pl.pallas_call(
        scatter_kernel,
        out_shape=(sds((NS, pad, width), BF), sds((NJ, 256, 128), wire)),
        in_specs=[ANY, VM],
        out_specs=[ANY, VM],
        scratch_shapes=[
            pltpu.VMEM((NJ, 256, 128), wire),
            pltpu.VMEM((NJ, 256, 128), wire),
            pltpu.VMEM((NY, 64, 128), F32),
            pltpu.VMEM((NY, 64, 128), F32),
            pltpu.VMEM((64, 128), wire),
            pltpu.VMEM((NZ, 64, 128), wire),
            pltpu.VMEM((NY, 64, 128), wire),
            dma(NJ), dma(NJ), dma(NY), dma(NY), dma(NZ), dma(NZ), dma(NY), dma(NY),
            dma(NS), dma(NS), dma(NJ), dma(NJ), pltpu.SemaphoreType.DMA,
        ],
        compiler_params=params(cid=2),
        name="scatter",
    )(c.reshape(NS, pad, width), g)
    parts = parts.reshape(NS // NY, rounds, pad, width)
    gt = grads + sum(parts[z].astype(F32) for z in range(NS // NY))
    g = g.astype(F32).reshape(4, 2, width, 128)
    g = jnp.concatenate([g[:, 0], g[:, 1]], axis=2)
    grad_tokens = jnp.swapaxes(gt[:, :rows], 0, 1)
    return (grad_tokens, g[0], g[1], g[2], g[3])


def solution(mesh):
    return jax.shard_map(
        shards,
        mesh=mesh,
        in_specs=(
            P("space", "tm", None),
            P(),
            P(),
            P(),
            P(),
            P("space", None),
            P("tm", None),
            P("space", "tm", None),
        ),
        out_specs=(P("space", "tm", None), P(), P(), P(), P()),
        check_vma=False,
    )
```

```python
import functools
import math

import jax
import jax.numpy as jnp
from jax import lax
from jax.experimental import pallas as pl
from jax.experimental.pallas import tpu as pltpu
from jax.sharding import PartitionSpec as P

HEADS = 8
NS = 16
NT = 16
NY = 4
NJ = 8
NZ = 8
MESH = pl.DeviceIdType.MESH
BF = jnp.bfloat16
F32 = jnp.float32
NEG = -1e30
MIB = 1 << 20

VM = pl.BlockSpec(memory_space=pltpu.VMEM)
ANY = pl.BlockSpec(memory_space=pl.ANY)


def params(mib=16, cid=None):
    if cid is None:
        return pltpu.CompilerParams(vmem_limit_bytes=mib * MIB)
    return pltpu.CompilerParams(
        vmem_limit_bytes=mib * MIB, collective_id=cid, has_side_effects=True
    )


def sds(shape, dtype):
    return jax.ShapeDtypeStruct(shape, dtype)


def nt(a, b):
    return lax.dot_general(a, b, (((1,), (1,)), ((), ())), preferred_element_type=F32)


def tn(a, b):
    return lax.dot_general(a, b, (((0,), (0,)), ((), ())), preferred_element_type=F32)


def nn(a, b):
    return jnp.dot(a, b, preferred_element_type=F32)


def mask_kernel(rows, pad, mask_ref, bias_ref):
    bias_ref[...] = jnp.full(bias_ref.shape, NEG, BF)
    bias = jnp.where(mask_ref[...] > 0, 0.0, NEG).astype(F32)
    for group in range(NS):
        bias_ref[0:rows, group * pad : group * pad + rows] = bias[
            :, group * rows : (group + 1) * rows
        ].astype(BF)


def attention_kernel(
    scale, x_ref, gb_ref, bias_ref, wq_ref, wk_ref, wv_ref, wo_ref, c_ref, g_ref,
    k_ref, v_ref, kt_ref, vt_ref, qt_ref, u_ref, ut_ref, q32, u32,
    s_ref, p_ref, pb_ref, t_ref, ds_ref, acc_q, acc_a, dkt, dvt,
):
    rows, width = gb_ref.shape
    size = width // HEADS
    half = width // 2
    first = pl.multiple_of(lax.axis_index("space") // NY * rows, rows)
    x = x_ref[...]
    xq = x_ref[pl.ds(first, rows), :]
    k_ref[...] = nn(x, wk_ref[...]).astype(BF)
    v_ref[...] = nn(x, wv_ref[...]).astype(BF)
    kt_ref[...] = nt(wk_ref[...].T, x).astype(BF)
    vt_ref[...] = nt(wv_ref[...].T, x).astype(BF)
    q = nn(xq, wq_ref[...]).astype(BF)
    qt_ref[...] = nt(wq_ref[...].T, xq).astype(BF)
    u_ref[...] = nt(gb_ref[...], wo_ref[...]).astype(BF)
    ut_ref[...] = nt(wo_ref[...], gb_ref[...]).astype(BF)
    for h in range(HEADS):
        q32[h] = q[:, h * size : (h + 1) * size]
        u32[h] = u_ref[:, h * size : (h + 1) * size]
    acc_q[...] = jnp.zeros_like(acc_q)
    acc_a[...] = jnp.zeros_like(acc_a)
    block, step = rows // 2, 16
    blocks = rows // block

    def head(h, carry):
        here = pl.ds(pl.multiple_of(h * size, size), size)
        own = lax.broadcasted_iota(jnp.int32, (block, width), 1) // size == h

        def scores(b):
            at = pl.ds(b * block, block)
            s_ref[at] = nn(q32[h, at, :], kt_ref[here, :])

        def slopes(b):
            at = pl.ds(b * block, block)
            t_ref[at] = nn(u32[h, at, :], vt_ref[here, :])

        def softmax(b):
            for i in range(block // step):
                at = pl.ds(b * block + i * step, step)
                z = s_ref[at, :] * scale + bias_ref[at, :].astype(F32)
                e = jnp.exp(z - jnp.max(z, axis=1, keepdims=True))
                p = e * (1.0 / jnp.sum(e, axis=1, keepdims=True))
                p_ref[at, :] = p
                pb_ref[at, :] = p.astype(BF)

        def attend(b):
            at = pl.ds(b * block, block)
            a = nn(pb_ref[at], v_ref[...]).astype(BF).astype(F32)
            a = jnp.where(own, a, 0.0)
            acc_a[at] += a
            return jnp.sum(u_ref[at].astype(F32) * a, axis=1, keepdims=True)

        def score_grads(b, deltas):
            for i in range(block // step):
                at = pl.ds(b * block + i * step, step)
                ds_ref[at, :] = (
                    p_ref[at, :] * (t_ref[at, :] - deltas[i * step : (i + 1) * step])
                ).astype(BF)
            at = pl.ds(b * block, block)
            acc_q[at] += jnp.where(own, nn(ds_ref[at], k_ref[...]), 0.0)

        scores(0)
        deltas = None
        for b in range(blocks):
            if b + 1 < blocks:
                scores(b + 1)
            slopes(b)
            softmax(b)
            if b > 0:
                score_grads(b - 1, deltas)
            deltas = attend(b)
        score_grads(blocks - 1, deltas)
        dkt[here, :] = nn(qt_ref[here, :], ds_ref[...])
        dvt[here, :] = nn(ut_ref[here, :], pb_ref[...])
        return carry

    lax.fori_loop(0, HEADS, head, 0)
    dq = (acc_q[...] * scale).astype(BF)
    dk = (dkt[...] * scale).astype(BF)
    dv = dvt[...].astype(BF)
    c_ref[...] = (nn(wk_ref[...], dk) + nn(wv_ref[...], dv)).T.astype(BF)
    own_rows = pl.ds(first, rows)
    back = nt(dq, wq_ref[...])
    c_ref[own_rows, :] = (c_ref[own_rows, :].astype(F32) + back).astype(BF)
    weights = (
        tn(xq, dq),
        nn(dk, x).T,
        nn(dv, x).T,
        tn(acc_a[...].astype(BF), gb_ref[...]),
    )
    for i, g in enumerate(weights):
        g_ref[2 * i] = g[:, 0:half]
        g_ref[2 * i + 1] = g[:, half:width]


def greet(diagonal):
    me = lax.axis_index("space")
    t = lax.axis_index("tm")
    y = lax.rem(me, NY)
    j = lax.rem(t, NJ)
    across = lax.rem(t + NJ, NT)
    far = range(1, NS // NY)
    peers = [{"space": me - y + lax.rem(y + k, NY)} for k in range(1, NY)]
    peers += [{"space": lax.rem(me + NY * k, NS)} for k in far]
    peers += [{"tm": t - j + lax.rem(j + k, NJ)} for k in range(1, NJ)]
    peers.append({"tm": across})
    if diagonal:
        peers += [{"tm": across, "space": lax.rem(me + NY * k, NS)} for k in far]
    barrier = pltpu.get_barrier_semaphore()
    for peer in peers:
        pl.semaphore_signal(barrier, inc=1, device_id=peer, device_id_type=MESH)
    return lambda: pl.semaphore_wait(barrier, len(peers))


def push(src, dst, sems, i, **to):
    return pltpu.make_async_remote_copy(
        src_ref=src,
        dst_ref=dst,
        send_sem=sems[0].at[i],
        recv_sem=sems[1].at[i],
        device_id=to,
        device_id_type=MESH,
    )


def gather_kernel(
    x_in, b_in, ct_ref, decay_ref, x_out, b_out, gb_out, grads_ref,
    got, late, late_in, gb_send, carried, run, prod, before,
    s0, r0, s1, r1, s2, r2, s3, r3, s4, r4, s5, r5, s6, r6, s7, r7, s8, r8, s9, r9, own,
):
    rounds, pad, _ = ct_ref.shape
    cols = b_in.shape[1] // 2
    me = lax.axis_index("space")
    y = lax.rem(me, NY)
    base = me - y
    depth = NS // NY
    z = lax.div(me, NY)
    right, left = lax.rem(z + 1, depth), lax.rem(z + depth - 1, depth)
    t = lax.axis_index("tm")
    core = lax.rem(t, 2)
    j = lax.rem(t, NJ)
    upper = t >= NJ
    half = pl.ds(pl.multiple_of(core * cols, cols), cols)
    all_here = greet(False)

    level = ct_ref[rounds - 1]
    reach = decay_ref[rounds - 1 : rounds, :]
    for r in range(rounds - 2, -1, -1):
        level = ct_ref[r] + decay_ref[r + 1 : r + 2, :] * level
        reach = reach * decay_ref[r : r + 1, :]
    got[j, 0:pad, :] = (decay_ref[0:1, :] * level).astype(BF)
    d0 = reach.astype(BF).astype(F32)
    d1 = (reach - d0).astype(BF).astype(F32)
    d2 = reach - d0 - d1
    row = lax.broadcasted_iota(jnp.int32, (16, reach.shape[1]), 0)
    got[j, pad : pad + 16, :] = jnp.where(row == 0, d0, jnp.where(row == 1, d1, d2)).astype(BF)

    all_here()
    scan = []
    for k in range(1, NJ):
        to = t - j + lax.rem(j + k, NJ)
        scan.append(push(got.at[j], got.at[j], (s3, r3), k, tm=to))
    tokens = []
    for k in range(1, NY):
        to = lax.rem(y + k, NY)
        tokens.append(push(x_in.at[to], x_out.at[me], (s0, r0), k, space=base + to))
    sides = []
    for k in range(NY):
        slot = base + lax.rem(y - k + NY, NY)
        src = x_in.at[y] if k == 0 else x_out.at[slot]
        sides.append(
            (
                push(src, x_out.at[slot], (s6, r6), k, space=right * NY + y),
                push(src, x_out.at[slot], (s7, r7), k, space=left * NY + y),
            )
        )
    passed = []
    for k in range(NY):
        of, to, sems = (left, right, (s8, r8)) if k < 2 else (right, left, (s9, r9))
        slot = x_out.at[of * NY + lax.rem(y - k + NY, NY)]
        passed.append(push(slot, slot, sems, k, space=to * NY + y))
    masks = []
    for k in range(1, NY):
        to = base + lax.rem(y + k, NY)
        masks.append(push(b_in.at[:, half], b_out.at[y, :, half], (s2, r2), k, space=to))
    local = [
        pltpu.make_async_copy(x_in.at[y], x_out.at[me], own.at[0]),
        pltpu.make_async_copy(b_in, b_out.at[y], own.at[1]),
    ]
    for copy in scan + tokens + list(sides[0]) + masks + local:
        copy.start()
    for k in range(1, NY):
        tokens[k - 1].wait()
        sides[k][0].start()
        sides[k][1].start()

    for copy in scan:
        copy.wait()
    run[...] = jnp.zeros(run.shape, F32)
    prod[...] = jnp.ones(prod.shape, F32)
    for i in range(NJ - 1, -1, -1):

        @pl.when(j == i)
        def _():
            carried[...] = run[...]
            before[...] = prod[...]

        tail = got[i, pad : pad + 16, :].astype(F32)
        step = tail[0:1] + tail[1:2] + tail[2:3]
        run[...] = got[i, 0:pad, :].astype(F32) + step * run[...]
        prod[...] = step * prod[...]
    late[...] = run[...].astype(BF)
    over = push(late, late_in, (s4, r4), 0, tm=lax.rem(t + NJ, NT))
    pl.when(upper)(over.start)
    for k in range(2):
        sides[k][0].wait()
        passed[k].start()

    @pl.when(jnp.logical_not(upper))
    def _():
        over.wait_recv()
        carried[...] += before[0:1, :] * late_in[...].astype(F32)

    level = ct_ref[rounds - 1] + carried[...]
    for r in range(rounds - 1, -1, -1):
        if r < rounds - 1:
            level = ct_ref[r] + decay_ref[r + 1 : r + 2, :] * level
        grads_ref[r] = level
        gb_send[r] = level.astype(BF)
    ups = []
    for k in range(1, NY):
        to = lax.rem(y + k, NY)
        ups.append(push(gb_send.at[to], gb_out.at[y], (s1, r1), k, space=base + to))
    ups.append(pltpu.make_async_copy(gb_send.at[y], gb_out.at[y], own.at[2]))
    for copy in ups:
        copy.start()

    shared = []
    for k in range(1, NY):
        masks[k - 1].wait()
        piece = b_out.at[lax.rem(y - k + NY, NY), :, half]
        copy = push(piece, piece, (s5, r5), k, tm=t + 1 - 2 * core)
        copy.start()
        shared.append(copy)
    for k in range(2, NY):
        sides[k][1].wait()
        passed[k].start()
    pl.when(upper)(over.wait_send)
    for copy in (sides[0][1], sides[1][1], sides[2][0], sides[3][0]):
        copy.wait()
    for copy in passed + local + ups + shared:
        copy.wait()


def scatter_kernel(
    c_in, g_in, c_out, g_out, send1, got1, part, got2, send3, got3, got4,
    far_l, far_r, mix_l, mix_r, got_l, got_r, sum_c, s0, r0, s1, r1, s2, r2, s3, r3, s4, r4, s5, r5, s6, r6,
):
    me = lax.axis_index("space")
    t = lax.axis_index("tm")
    y = lax.rem(me, NY)
    base = me - y
    j = lax.rem(t, NJ)
    z = lax.div(me, NY)
    depth = NS // NY
    right, left, opposite = (lax.rem(z + k, depth) for k in (1, depth - 1, 2))
    line = z * 2 + lax.div(t, NJ)
    all_here = greet(True)
    for i in range(NJ):
        send1[i] = g_in[i].astype(send1.dtype)
    all_here()

    first = []
    for k in range(1, NJ):
        to = lax.rem(j + k, NJ)
        first.append(push(send1.at[to], got1.at[j], (s0, r0), k, tm=t - j + to))
    two = 2
    far = [
        push(c_in.at[pl.ds(opposite * NY, two)], far_l, (s4, r4), 0, space=right * NY + y),
        push(c_in.at[pl.ds(opposite * NY + two, two)], far_r, (s4, r4), 1, space=left * NY + y),
    ]
    near = [
        push(
            c_in.at[pl.ds(right * NY + two, two)], got_l.at[pl.ds(two, two)], (s4, r4), 2,
            space=right * NY + y,
        ),
        push(
            c_in.at[pl.ds(left * NY, two)], got_r.at[pl.ds(0, two)], (s4, r4), 3,
            space=left * NY + y,
        ),
    ]
    for copy in far + first + near:
        copy.start()
    mixed = [
        push(mix_r, got_l.at[pl.ds(0, two)], (s4, r4), 4, space=right * NY + y),
        push(mix_l, got_r.at[pl.ds(two, two)], (s4, r4), 5, space=left * NY + y),
    ]
    far[0].wait()
    for i in range(two):
        mix_r[i] = (c_in[right * NY + i].astype(F32) + far_l[i].astype(F32)).astype(BF)
    mixed[0].start()
    far[1].wait()
    for i in range(two):
        mix_l[i] = (c_in[left * NY + two + i].astype(F32) + far_r[i].astype(F32)).astype(BF)
    mixed[1].start()
    total = g_in[j]
    for copy in first:
        copy.wait()
    for k in range(1, NJ):
        total = total + got1[lax.rem(j + k, NJ)].astype(F32)
    part[...] = total.reshape(part.shape)

    second = []
    for k in range(1, NY):
        to = lax.rem(y + k, NY)
        second.append(push(part.at[to], got2.at[y], (s1, r1), k, space=base + to))
    for copy in second:
        copy.start()
    total = part[y]
    for copy in second:
        copy.wait()
    for k in range(1, NY):
        total = total + got2[lax.rem(y + k, NY)]
    send3[...] = total.astype(send3.dtype)
    got3[line] = send3[...]

    third = []
    for k in range(1, NZ):
        to = lax.rem(line + k, NZ)
        third.append(
            push(
                send3, got3.at[line], (s2, r2), k,
                tm=lax.rem(to, 2) * NJ + j, space=lax.div(to, 2) * NY + y,
            )
        )
    for copy in third:
        copy.start()
    for copy in third:
        copy.wait()
    total = got3[0].astype(F32)
    for i in range(1, NZ):
        total = total + got3[i].astype(F32)
    got4[y] = total.astype(got4.dtype)

    fourth = []
    for k in range(1, NY):
        to = base + lax.rem(y + k, NY)
        fourth.append(push(got4.at[y], got4.at[y], (s3, r3), k, space=to))
    for copy in fourth:
        copy.start()
    for copy in near + mixed:
        copy.wait()
    for i in range(NY):
        block = c_in[z * NY + i].astype(F32) + got_l[i].astype(F32) + got_r[i].astype(F32)
        sum_c[i] = block.astype(BF)
    tokens = []
    for k in range(1, NY):
        to = lax.rem(y + k, NY)
        tokens.append(push(sum_c.at[to], c_out.at[y], (s6, r6), k, space=base + to))
    for copy in tokens:
        copy.start()
    c_out[y] = sum_c[y]
    for copy in fourth:
        copy.wait()
    g_out[j] = got4[...].reshape(g_out.shape[1:])

    fifth = []
    for k in range(1, NJ):
        to = t - j + lax.rem(j + k, NJ)
        fifth.append(push(g_out.at[j], g_out.at[j], (s5, r5), k, tm=to))
    for copy in fifth:
        copy.start()
    for copy in fifth + tokens:
        copy.wait()


def dma(n):
    return pltpu.SemaphoreType.DMA((n,))


def shards(tokens, w_query, w_key, w_value, w_out, mask, decay, cotangent):
    rows, rounds, width = tokens.shape
    pad = -(-rows // 16) * 16
    keys = NS * pad
    quads = NY * pad
    size = width // HEADS
    scale = 1.0 / math.sqrt(size)

    bias = pl.pallas_call(
        functools.partial(mask_kernel, rows, pad),
        out_shape=sds((pad, keys), BF),
        in_specs=[VM],
        out_specs=VM,
        compiler_params=params(),
        name="mask_rows",
    )(mask)
    widen = ((0, 0), (0, pad - rows), (0, 0))
    x = jnp.pad(jnp.swapaxes(tokens, 0, 1), widen)
    ct = jnp.pad(jnp.swapaxes(cotangent, 0, 1), widen)

    x_all, bias_all, gb_all, grads = pl.pallas_call(
        gather_kernel,
        out_shape=(
            sds((NS, pad, width), BF),
            sds((NY, pad, keys), BF),
            sds((NY, pad, width), BF),
            sds((rounds, pad, width), F32),
        ),
        in_specs=[ANY, ANY, VM, VM],
        out_specs=[ANY, ANY, ANY, VM],
        scratch_shapes=[
            pltpu.VMEM((NJ, pad + 16, width), BF),
            pltpu.VMEM((pad, width), BF),
            pltpu.VMEM((pad, width), BF),
            pltpu.VMEM((rounds, pad, width), BF),
            pltpu.VMEM((pad, width), F32),
            pltpu.VMEM((pad, width), F32),
            pltpu.VMEM((8, width), F32),
            pltpu.VMEM((8, width), F32),
            dma(NY), dma(NY), dma(NY), dma(NY), dma(NY), dma(NY),
            dma(NJ), dma(NJ), dma(1), dma(1), dma(NY), dma(NY),
            dma(NY), dma(NY), dma(NY), dma(NY), dma(NY), dma(NY), dma(NY), dma(NY), dma(3),
        ],
        compiler_params=params(cid=1),
        name="gather",
    )(x, bias, ct, decay)

    c, g = pl.pallas_call(
        functools.partial(attention_kernel, scale),
        out_shape=(sds((keys, width), BF), sds((8, width, width // 2), F32)),
        in_specs=[VM] * 7,
        out_specs=[VM] * 2,
        scratch_shapes=[
            pltpu.VMEM((keys, width), BF),
            pltpu.VMEM((keys, width), BF),
            pltpu.VMEM((width, keys), BF),
            pltpu.VMEM((width, keys), BF),
            pltpu.VMEM((width, quads), BF),
            pltpu.VMEM((quads, width), BF),
            pltpu.VMEM((width, quads), BF),
            pltpu.VMEM((HEADS, quads, size), BF),
            pltpu.VMEM((HEADS, quads, size), BF),
            pltpu.VMEM((quads, keys), F32),
            pltpu.VMEM((quads, keys), F32),
            pltpu.VMEM((quads, keys), BF),
            pltpu.VMEM((quads, keys), F32),
            pltpu.VMEM((quads, keys), BF),
            pltpu.VMEM((quads, width), F32),
            pltpu.VMEM((quads, width), F32),
            pltpu.VMEM((width, keys), F32),
            pltpu.VMEM((width, keys), F32),
        ],
        compiler_params=params(42),
        name="attention",
    )(
        x_all.reshape(keys, width),
        gb_all.reshape(quads, width),
        bias_all.reshape(quads, keys),
        w_query, w_key, w_value, w_out,
    )

    wire = BF
    parts, g = pl.pallas_call(
        scatter_kernel,
        out_shape=(sds((rounds, pad, width), BF), sds((NJ, 256, 128), wire)),
        in_specs=[VM, VM],
        out_specs=[VM, VM],
        scratch_shapes=[
            pltpu.VMEM((NJ, 256, 128), wire),
            pltpu.VMEM((NJ, 256, 128), wire),
            pltpu.VMEM((NY, 64, 128), F32),
            pltpu.VMEM((NY, 64, 128), F32),
            pltpu.VMEM((64, 128), wire),
            pltpu.VMEM((NZ, 64, 128), wire),
            pltpu.VMEM((NY, 64, 128), wire),
            pltpu.VMEM((2, pad, width), BF),
            pltpu.VMEM((2, pad, width), BF),
            pltpu.VMEM((2, pad, width), BF),
            pltpu.VMEM((2, pad, width), BF),
            pltpu.VMEM((NY, pad, width), BF),
            pltpu.VMEM((NY, pad, width), BF),
            pltpu.VMEM((NY, pad, width), BF),
            dma(NJ), dma(NJ), dma(NY), dma(NY), dma(NZ), dma(NZ), dma(NY), dma(NY),
            dma(6), dma(6), dma(NJ), dma(NJ), dma(NY), dma(NY),
        ],
        compiler_params=params(cid=2),
        name="scatter",
    )(c.reshape(NS, pad, width), g)
    gt = grads + parts.astype(F32)
    g = g.astype(F32).reshape(4, 2, width, 128)
    g = jnp.concatenate([g[:, 0], g[:, 1]], axis=2)
    grad_tokens = jnp.swapaxes(gt[:, :rows], 0, 1)
    return (grad_tokens, g[0], g[1], g[2], g[3])


def solution(mesh):
    return jax.shard_map(
        shards,
        mesh=mesh,
        in_specs=(
            P("space", "tm", None),
            P(),
            P(),
            P(),
            P(),
            P("space", None),
            P("tm", None),
            P("space", "tm", None),
        ),
        out_specs=(P("space", "tm", None), P(), P(), P(), P()),
        check_vma=False,
    )
```

```python
import functools
import math

import jax
import jax.numpy as jnp
from jax import lax
from jax.experimental import pallas as pl
from jax.experimental.pallas import tpu as pltpu
from jax.sharding import PartitionSpec as P

HEADS = 8
NS = 16
NT = 16
NY = 4
NJ = 8
NZ = 8
MESH = pl.DeviceIdType.MESH
BF = jnp.bfloat16
F32 = jnp.float32
NEG = -1e30
MIB = 1 << 20

VM = pl.BlockSpec(memory_space=pltpu.VMEM)
ANY = pl.BlockSpec(memory_space=pl.ANY)


def params(mib=16, cid=None):
    if cid is None:
        return pltpu.CompilerParams(vmem_limit_bytes=mib * MIB)
    return pltpu.CompilerParams(
        vmem_limit_bytes=mib * MIB, collective_id=cid, has_side_effects=True
    )


def sds(shape, dtype):
    return jax.ShapeDtypeStruct(shape, dtype)


def nt(a, b):
    return lax.dot_general(a, b, (((1,), (1,)), ((), ())), preferred_element_type=F32)


def tn(a, b):
    return lax.dot_general(a, b, (((0,), (0,)), ((), ())), preferred_element_type=F32)


def nn(a, b):
    return jnp.dot(a, b, preferred_element_type=F32)


def attention_kernel(
    scale, x_ref, gb_ref, bias_ref, wq_ref, wk_ref, wv_ref, wo_ref, c_ref, g_ref,
    k_ref, v_ref, kt_ref, vt_ref, qt_ref, u_ref, ut_ref, q32, u32,
    s_ref, p_ref, pb_ref, t_ref, ds_ref, acc_q, acc_a, dkt, dvt,
):
    rows, width = gb_ref.shape
    size = width // HEADS
    half = width // 2
    first = pl.multiple_of(lax.axis_index("space") // NY * rows, rows)
    x = x_ref[...]
    xq = x_ref[pl.ds(first, rows), :]
    k_ref[...] = nn(x, wk_ref[...]).astype(BF)
    v_ref[...] = nn(x, wv_ref[...]).astype(BF)
    kt_ref[...] = nt(wk_ref[...].T, x).astype(BF)
    vt_ref[...] = nt(wv_ref[...].T, x).astype(BF)
    q = nn(xq, wq_ref[...]).astype(BF)
    qt_ref[...] = nt(wq_ref[...].T, xq).astype(BF)
    u_ref[...] = nt(gb_ref[...], wo_ref[...]).astype(BF)
    ut_ref[...] = nt(wo_ref[...], gb_ref[...]).astype(BF)
    for h in range(HEADS):
        q32[h] = q[:, h * size : (h + 1) * size]
        u32[h] = u_ref[:, h * size : (h + 1) * size]
    acc_q[...] = jnp.zeros_like(acc_q)
    acc_a[...] = jnp.zeros_like(acc_a)
    block, step = rows // 2, 16
    blocks = rows // block

    def head(h, carry):
        here = pl.ds(pl.multiple_of(h * size, size), size)
        own = lax.broadcasted_iota(jnp.int32, (block, width), 1) // size == h

        def scores(b):
            at = pl.ds(b * block, block)
            s_ref[at] = nn(q32[h, at, :], kt_ref[here, :])

        def slopes(b):
            at = pl.ds(b * block, block)
            t_ref[at] = nn(u32[h, at, :], vt_ref[here, :])

        def softmax(b):
            for i in range(block // step):
                at = pl.ds(b * block + i * step, step)
                z = s_ref[at, :] * scale + bias_ref[at, :].astype(F32)
                e = jnp.exp(z - jnp.max(z, axis=1, keepdims=True))
                p = e * (1.0 / jnp.sum(e, axis=1, keepdims=True))
                p_ref[at, :] = p
                pb_ref[at, :] = p.astype(BF)

        def attend(b):
            at = pl.ds(b * block, block)
            a = nn(pb_ref[at], v_ref[...]).astype(BF).astype(F32)
            a = jnp.where(own, a, 0.0)
            acc_a[at] += a
            return jnp.sum(u_ref[at].astype(F32) * a, axis=1, keepdims=True)

        def score_grads(b, deltas):
            for i in range(block // step):
                at = pl.ds(b * block + i * step, step)
                ds_ref[at, :] = (
                    p_ref[at, :] * (t_ref[at, :] - deltas[i * step : (i + 1) * step])
                ).astype(BF)
            at = pl.ds(b * block, block)
            acc_q[at] += jnp.where(own, nn(ds_ref[at], k_ref[...]), 0.0)

        scores(0)
        deltas = None
        for b in range(blocks):
            if b + 1 < blocks:
                scores(b + 1)
            slopes(b)
            softmax(b)
            if b > 0:
                score_grads(b - 1, deltas)
            deltas = attend(b)
        score_grads(blocks - 1, deltas)
        dkt[here, :] = nn(qt_ref[here, :], ds_ref[...])
        dvt[here, :] = nn(ut_ref[here, :], pb_ref[...])
        return carry

    lax.fori_loop(0, HEADS, head, 0)
    dq = (acc_q[...] * scale).astype(BF)
    dk = (dkt[...] * scale).astype(BF)
    dv = dvt[...].astype(BF)
    c_ref[...] = (nn(wk_ref[...], dk) + nn(wv_ref[...], dv)).T.astype(BF)
    own_rows = pl.ds(first, rows)
    back = nt(dq, wq_ref[...])
    c_ref[own_rows, :] = (c_ref[own_rows, :].astype(F32) + back).astype(BF)
    weights = (
        tn(xq, dq),
        nn(dk, x).T,
        nn(dv, x).T,
        tn(acc_a[...].astype(BF), gb_ref[...]),
    )
    for i, g in enumerate(weights):
        g_ref[2 * i] = g[:, 0:half]
        g_ref[2 * i + 1] = g[:, half:width]


def greet(diagonal):
    me = lax.axis_index("space")
    t = lax.axis_index("tm")
    y = lax.rem(me, NY)
    j = lax.rem(t, NJ)
    across = lax.rem(t + NJ, NT)
    far = range(1, NS // NY)
    peers = [{"space": me - y + lax.rem(y + k, NY)} for k in range(1, NY)]
    peers += [{"space": lax.rem(me + NY * k, NS)} for k in far]
    peers += [{"tm": t - j + lax.rem(j + k, NJ)} for k in range(1, NJ)]
    peers.append({"tm": across})
    if diagonal:
        peers += [{"tm": across, "space": lax.rem(me + NY * k, NS)} for k in far]
    barrier = pltpu.get_barrier_semaphore()
    for peer in peers:
        pl.semaphore_signal(barrier, inc=1, device_id=peer, device_id_type=MESH)
    return lambda: pl.semaphore_wait(barrier, len(peers))


def push(src, dst, sems, i, **to):
    return pltpu.make_async_remote_copy(
        src_ref=src,
        dst_ref=dst,
        send_sem=sems[0].at[i],
        recv_sem=sems[1].at[i],
        device_id=to,
        device_id_type=MESH,
    )


def gather_kernel(
    rows, x_in, mask_ref, ct_ref, decay_ref, x_out, b_out, gb_out, grads_ref,
    b_in, got, late, late_in, gb_send, carried, run, prod, before,
    s0, r0, s1, r1, s2, r2, s3, r3, s4, r4, s5, r5, s6, r6, s7, r7, s8, r8, s9, r9, own,
):
    rounds, pad, _ = ct_ref.shape
    cols = b_in.shape[1] // 2
    me = lax.axis_index("space")
    y = lax.rem(me, NY)
    base = me - y
    depth = NS // NY
    z = lax.div(me, NY)
    right, left = lax.rem(z + 1, depth), lax.rem(z + depth - 1, depth)
    t = lax.axis_index("tm")
    core = lax.rem(t, 2)
    j = lax.rem(t, NJ)
    upper = t >= NJ
    half = pl.ds(pl.multiple_of(core * cols, cols), cols)
    all_here = greet(False)
    level = ct_ref[rounds - 1]
    reach = decay_ref[rounds - 1 : rounds, :]
    for r in range(rounds - 2, -1, -1):
        level = ct_ref[r] + decay_ref[r + 1 : r + 2, :] * level
        reach = reach * decay_ref[r : r + 1, :]
    got[j, 0:pad, :] = (decay_ref[0:1, :] * level).astype(BF)
    d0 = reach.astype(BF).astype(F32)
    d1 = (reach - d0).astype(BF).astype(F32)
    d2 = reach - d0 - d1
    row = lax.broadcasted_iota(jnp.int32, (16, reach.shape[1]), 0)
    got[j, pad : pad + 16, :] = jnp.where(row == 0, d0, jnp.where(row == 1, d1, d2)).astype(BF)

    b_in[...] = jnp.full(b_in.shape, NEG, BF)
    bias = jnp.where(mask_ref[...] > 0, 0.0, NEG).astype(F32)
    for group in range(NS):
        b_in[0:rows, group * pad : group * pad + rows] = bias[
            :, group * rows : (group + 1) * rows
        ].astype(BF)

    all_here()
    scan = []
    for k in range(1, NJ):
        to = t - j + lax.rem(j + k, NJ)
        scan.append(push(got.at[j], got.at[j], (s3, r3), k, tm=to))
    tokens = []
    for k in range(1, NY):
        to = lax.rem(y + k, NY)
        tokens.append(push(x_in.at[to], x_out.at[me], (s0, r0), k, space=base + to))
    sides = []
    for k in range(NY):
        slot = base + lax.rem(y - k + NY, NY)
        src = x_in.at[y] if k == 0 else x_out.at[slot]
        sides.append(
            (
                push(src, x_out.at[slot], (s6, r6), k, space=right * NY + y),
                push(src, x_out.at[slot], (s7, r7), k, space=left * NY + y),
            )
        )
    passed = []
    for k in range(NY):
        of, to, sems = (left, right, (s8, r8)) if k < 2 else (right, left, (s9, r9))
        slot = x_out.at[of * NY + lax.rem(y - k + NY, NY)]
        passed.append(push(slot, slot, sems, k, space=to * NY + y))
    masks = []
    for k in range(1, NY):
        to = base + lax.rem(y + k, NY)
        masks.append(push(b_in.at[:, half], b_out.at[y, :, half], (s2, r2), k, space=to))
    local = [
        pltpu.make_async_copy(x_in.at[y], x_out.at[me], own.at[0]),
        pltpu.make_async_copy(b_in, b_out.at[y], own.at[1]),
    ]
    for copy in list(sides[0]) + tokens + scan + masks + local:
        copy.start()
    for k in range(1, NY):
        tokens[k - 1].wait()
        sides[k][0].start()
        sides[k][1].start()

    for copy in scan:
        copy.wait()
    run[...] = jnp.zeros(run.shape, F32)
    prod[...] = jnp.ones(prod.shape, F32)
    for i in range(NJ - 1, -1, -1):

        @pl.when(j == i)
        def _():
            carried[...] = run[...]
            before[...] = prod[...]

        tail = got[i, pad : pad + 16, :].astype(F32)
        step = tail[0:1] + tail[1:2] + tail[2:3]
        run[...] = got[i, 0:pad, :].astype(F32) + step * run[...]
        prod[...] = step * prod[...]
    late[...] = run[...].astype(BF)
    over = push(late, late_in, (s4, r4), 0, tm=lax.rem(t + NJ, NT))
    pl.when(upper)(over.start)
    for k in range(3):
        sides[k][0 if k < 2 else 1].wait()
        passed[k].start()

    @pl.when(jnp.logical_not(upper))
    def _():
        over.wait_recv()
        carried[...] += before[0:1, :] * late_in[...].astype(F32)

    level = ct_ref[rounds - 1] + carried[...]
    for r in range(rounds - 1, -1, -1):
        if r < rounds - 1:
            level = ct_ref[r] + decay_ref[r + 1 : r + 2, :] * level
        grads_ref[r] = level
        gb_send[r] = level.astype(BF)
    ups = []
    for k in range(1, NY):
        to = lax.rem(y + k, NY)
        ups.append(push(gb_send.at[to], gb_out.at[y], (s1, r1), k, space=base + to))
    ups.append(pltpu.make_async_copy(gb_send.at[y], gb_out.at[y], own.at[2]))
    for copy in ups:
        copy.start()

    sides[3][1].wait()
    passed[3].start()
    shared = []
    for k in range(1, NY):
        masks[k - 1].wait()
        piece = b_out.at[lax.rem(y - k + NY, NY), :, half]
        copy = push(piece, piece, (s5, r5), k, tm=t + 1 - 2 * core)
        copy.start()
        shared.append(copy)
    pl.when(upper)(over.wait_send)
    for copy in (sides[0][1], sides[1][1], sides[2][0], sides[3][0]):
        copy.wait()
    for copy in passed + local + ups + shared:
        copy.wait()


def scatter_kernel(
    c_in, g_in, c_out, g_out, send1, got1, part, send2, got2, send3, got3, got4,
    far_l, far_r, mix_l, mix_r, got_l, got_r, sum_c, s0, r0, s1, r1, s2, r2, s3, r3, s4, r4, s5, r5, s6, r6,
):
    me = lax.axis_index("space")
    t = lax.axis_index("tm")
    y = lax.rem(me, NY)
    base = me - y
    j = lax.rem(t, NJ)
    z = lax.div(me, NY)
    depth = NS // NY
    right, left, opposite = (lax.rem(z + k, depth) for k in (1, depth - 1, 2))
    line = z * 2 + lax.div(t, NJ)
    all_here = greet(True)
    for i in range(NJ):
        send1[i] = g_in[i].astype(send1.dtype)
    all_here()

    first = []
    for k in range(1, NJ):
        to = lax.rem(j + k, NJ)
        first.append(push(send1.at[to], got1.at[j], (s0, r0), k, tm=t - j + to))
    two = 2
    far = [
        push(c_in.at[pl.ds(opposite * NY, two)], far_l, (s4, r4), 0, space=right * NY + y),
        push(c_in.at[pl.ds(opposite * NY + two, two)], far_r, (s4, r4), 1, space=left * NY + y),
    ]
    near = [
        push(
            c_in.at[pl.ds(right * NY + two, two)], got_l.at[pl.ds(two, two)], (s4, r4), 2,
            space=right * NY + y,
        ),
        push(
            c_in.at[pl.ds(left * NY, two)], got_r.at[pl.ds(0, two)], (s4, r4), 3,
            space=left * NY + y,
        ),
    ]
    for copy in far + first + near:
        copy.start()
    mixed = [
        push(mix_r, got_l.at[pl.ds(0, two)], (s4, r4), 4, space=right * NY + y),
        push(mix_l, got_r.at[pl.ds(two, two)], (s4, r4), 5, space=left * NY + y),
    ]
    total = g_in[j]
    for copy in first:
        copy.wait()
    for k in range(1, NJ):
        total = total + got1[lax.rem(j + k, NJ)].astype(F32)
    part[...] = total.reshape(part.shape)
    send2[...] = part[...].astype(send2.dtype)

    second = []
    for k in range(1, NY):
        to = lax.rem(y + k, NY)
        second.append(push(send2.at[to], got2.at[y], (s1, r1), k, space=base + to))
    for copy in second:
        copy.start()
    far[0].wait()
    for i in range(two):
        mix_r[i] = (c_in[right * NY + i].astype(F32) + far_l[i].astype(F32)).astype(BF)
    mixed[0].start()
    far[1].wait()
    for i in range(two):
        mix_l[i] = (c_in[left * NY + two + i].astype(F32) + far_r[i].astype(F32)).astype(BF)
    mixed[1].start()
    total = part[y]
    for copy in second:
        copy.wait()
    for k in range(1, NY):
        total = total + got2[lax.rem(y + k, NY)].astype(F32)
    send3[...] = total.astype(send3.dtype)
    got3[line] = send3[...]

    third = []
    for k in range(1, NZ):
        to = lax.rem(line + k, NZ)
        third.append(
            push(
                send3, got3.at[line], (s2, r2), k,
                tm=lax.rem(to, 2) * NJ + j, space=lax.div(to, 2) * NY + y,
            )
        )
    for copy in third:
        copy.start()
    for copy in third:
        copy.wait()
    total = got3[0].astype(F32)
    for i in range(1, NZ):
        total = total + got3[i].astype(F32)
    got4[y] = total.astype(got4.dtype)

    fourth = []
    for k in range(1, NY):
        to = base + lax.rem(y + k, NY)
        fourth.append(push(got4.at[y], got4.at[y], (s3, r3), k, space=to))
    for copy in fourth:
        copy.start()
    for copy in fourth:
        copy.wait()
    g_out[j] = got4[...].reshape(g_out.shape[1:])

    fifth = []
    for k in range(1, NJ):
        to = t - j + lax.rem(j + k, NJ)
        fifth.append(push(g_out.at[j], g_out.at[j], (s5, r5), k, tm=to))
    for copy in fifth:
        copy.start()
    for copy in near + mixed:
        copy.wait()
    for i in range(NY):
        block = c_in[z * NY + i].astype(F32) + got_l[i].astype(F32) + got_r[i].astype(F32)
        sum_c[i] = block.astype(BF)
    tokens = []
    for k in range(1, NY):
        to = lax.rem(y + k, NY)
        tokens.append(push(sum_c.at[to], c_out.at[y], (s6, r6), k, space=base + to))
    for copy in tokens:
        copy.start()
    c_out[y] = sum_c[y]
    for copy in fifth + tokens:
        copy.wait()


def dma(n):
    return pltpu.SemaphoreType.DMA((n,))


def shards(tokens, w_query, w_key, w_value, w_out, mask, decay, cotangent):
    rows, rounds, width = tokens.shape
    pad = -(-rows // 16) * 16
    keys = NS * pad
    quads = NY * pad
    size = width // HEADS
    scale = 1.0 / math.sqrt(size)

    widen = ((0, 0), (0, pad - rows), (0, 0))
    x = jnp.pad(jnp.swapaxes(tokens, 0, 1), widen)
    ct = jnp.pad(jnp.swapaxes(cotangent, 0, 1), widen)

    x_all, bias_all, gb_all, grads = pl.pallas_call(
        functools.partial(gather_kernel, rows),
        out_shape=(
            sds((NS, pad, width), BF),
            sds((NY, pad, keys), BF),
            sds((NY, pad, width), BF),
            sds((rounds, pad, width), F32),
        ),
        in_specs=[ANY, VM, VM, VM],
        out_specs=[ANY, ANY, ANY, VM],
        scratch_shapes=[
            pltpu.VMEM((pad, keys), BF),
            pltpu.VMEM((NJ, pad + 16, width), BF),
            pltpu.VMEM((pad, width), BF),
            pltpu.VMEM((pad, width), BF),
            pltpu.VMEM((rounds, pad, width), BF),
            pltpu.VMEM((pad, width), F32),
            pltpu.VMEM((pad, width), F32),
            pltpu.VMEM((8, width), F32),
            pltpu.VMEM((8, width), F32),
            dma(NY), dma(NY), dma(NY), dma(NY), dma(NY), dma(NY),
            dma(NJ), dma(NJ), dma(1), dma(1), dma(NY), dma(NY),
            dma(NY), dma(NY), dma(NY), dma(NY), dma(NY), dma(NY), dma(NY), dma(NY), dma(3),
        ],
        compiler_params=params(cid=1),
        name="gather",
    )(x, mask, ct, decay)

    c, g = pl.pallas_call(
        functools.partial(attention_kernel, scale),
        out_shape=(sds((keys, width), BF), sds((8, width, width // 2), F32)),
        in_specs=[VM] * 7,
        out_specs=[VM] * 2,
        scratch_shapes=[
            pltpu.VMEM((keys, width), BF),
            pltpu.VMEM((keys, width), BF),
            pltpu.VMEM((width, keys), BF),
            pltpu.VMEM((width, keys), BF),
            pltpu.VMEM((width, quads), BF),
            pltpu.VMEM((quads, width), BF),
            pltpu.VMEM((width, quads), BF),
            pltpu.VMEM((HEADS, quads, size), BF),
            pltpu.VMEM((HEADS, quads, size), BF),
            pltpu.VMEM((quads, keys), F32),
            pltpu.VMEM((quads, keys), F32),
            pltpu.VMEM((quads, keys), BF),
            pltpu.VMEM((quads, keys), F32),
            pltpu.VMEM((quads, keys), BF),
            pltpu.VMEM((quads, width), F32),
            pltpu.VMEM((quads, width), F32),
            pltpu.VMEM((width, keys), F32),
            pltpu.VMEM((width, keys), F32),
        ],
        compiler_params=params(42),
        name="attention",
    )(
        x_all.reshape(keys, width),
        gb_all.reshape(quads, width),
        bias_all.reshape(quads, keys),
        w_query, w_key, w_value, w_out,
    )

    wire = BF
    parts, g = pl.pallas_call(
        scatter_kernel,
        out_shape=(sds((rounds, pad, width), BF), sds((NJ, 256, 128), wire)),
        in_specs=[VM, VM],
        out_specs=[VM, VM],
        scratch_shapes=[
            pltpu.VMEM((NJ, 256, 128), wire),
            pltpu.VMEM((NJ, 256, 128), wire),
            pltpu.VMEM((NY, 64, 128), F32),
            pltpu.VMEM((NY, 64, 128), wire),
            pltpu.VMEM((NY, 64, 128), wire),
            pltpu.VMEM((64, 128), wire),
            pltpu.VMEM((NZ, 64, 128), wire),
            pltpu.VMEM((NY, 64, 128), wire),
            pltpu.VMEM((2, pad, width), BF),
            pltpu.VMEM((2, pad, width), BF),
            pltpu.VMEM((2, pad, width), BF),
            pltpu.VMEM((2, pad, width), BF),
            pltpu.VMEM((NY, pad, width), BF),
            pltpu.VMEM((NY, pad, width), BF),
            pltpu.VMEM((NY, pad, width), BF),
            dma(NJ), dma(NJ), dma(NY), dma(NY), dma(NZ), dma(NZ), dma(NY), dma(NY),
            dma(6), dma(6), dma(NJ), dma(NJ), dma(NY), dma(NY),
        ],
        compiler_params=params(cid=2),
        name="scatter",
    )(c.reshape(NS, pad, width), g)
    gt = grads + parts.astype(F32)
    g = g.astype(F32).reshape(4, 2, width, 128)
    g = jnp.concatenate([g[:, 0], g[:, 1]], axis=2)
    grad_tokens = jnp.swapaxes(gt[:, :rows], 0, 1)
    return (grad_tokens, g[0], g[1], g[2], g[3])


def solution(mesh):
    return jax.shard_map(
        shards,
        mesh=mesh,
        in_specs=(
            P("space", "tm", None),
            P(),
            P(),
            P(),
            P(),
            P("space", None),
            P("tm", None),
            P("space", "tm", None),
        ),
        out_specs=(P("space", "tm", None), P(), P(), P(), P()),
        check_vma=False,
    )
```

```python
import functools
import math

import jax
import jax.numpy as jnp
from jax import lax
from jax.experimental import pallas as pl
from jax.experimental.pallas import tpu as pltpu
from jax.sharding import PartitionSpec as P

HEADS = 8
NS = 16
NT = 16
NY = 4
NJ = 8
NZ = 8
MESH = pl.DeviceIdType.MESH
BF = jnp.bfloat16
F32 = jnp.float32
NEG = -1e30
MIB = 1 << 20

VM = pl.BlockSpec(memory_space=pltpu.VMEM)
ANY = pl.BlockSpec(memory_space=pl.ANY)


def params(mib=16, cid=None):
    if cid is None:
        return pltpu.CompilerParams(vmem_limit_bytes=mib * MIB)
    return pltpu.CompilerParams(
        vmem_limit_bytes=mib * MIB, collective_id=cid, has_side_effects=True
    )


def sds(shape, dtype):
    return jax.ShapeDtypeStruct(shape, dtype)


def nt(a, b):
    return lax.dot_general(a, b, (((1,), (1,)), ((), ())), preferred_element_type=F32)


def tn(a, b):
    return lax.dot_general(a, b, (((0,), (0,)), ((), ())), preferred_element_type=F32)


def nn(a, b):
    return jnp.dot(a, b, preferred_element_type=F32)


def attention_kernel(
    scale, x_ref, gb_ref, bias_ref, wq_ref, wk_ref, wv_ref, wo_ref, c_ref, g_ref,
    k_ref, v_ref, kt_ref, vt_ref, qt_ref, u_ref, ut_ref, q32, u32,
    s_ref, p_ref, pb_ref, t_ref, ds_ref, acc_q, acc_a, dkt, dvt,
):
    rows, width = gb_ref.shape
    size = width // HEADS
    half = width // 2
    first = pl.multiple_of(lax.axis_index("space") // NY * rows, rows)
    x = x_ref[...]
    xq = x_ref[pl.ds(first, rows), :]
    k_ref[...] = nn(x, wk_ref[...]).astype(BF)
    v_ref[...] = nn(x, wv_ref[...]).astype(BF)
    kt_ref[...] = nt(wk_ref[...].T, x).astype(BF)
    vt_ref[...] = nt(wv_ref[...].T, x).astype(BF)
    q = nn(xq, wq_ref[...]).astype(BF)
    qt_ref[...] = nt(wq_ref[...].T, xq).astype(BF)
    u_ref[...] = nt(gb_ref[...], wo_ref[...]).astype(BF)
    ut_ref[...] = nt(wo_ref[...], gb_ref[...]).astype(BF)
    for h in range(HEADS):
        q32[h] = q[:, h * size : (h + 1) * size]
        u32[h] = u_ref[:, h * size : (h + 1) * size]
    acc_q[...] = jnp.zeros_like(acc_q)
    acc_a[...] = jnp.zeros_like(acc_a)
    block, step = rows // 2, 16
    blocks = rows // block

    def head(h, carry):
        here = pl.ds(pl.multiple_of(h * size, size), size)
        own = lax.broadcasted_iota(jnp.int32, (block, width), 1) // size == h

        def scores(b):
            at = pl.ds(b * block, block)
            s_ref[at] = nn(q32[h, at, :], kt_ref[here, :])

        def slopes(b):
            at = pl.ds(b * block, block)
            t_ref[at] = nn(u32[h, at, :], vt_ref[here, :])

        def softmax(b):
            for i in range(block // step):
                at = pl.ds(b * block + i * step, step)
                z = s_ref[at, :] * scale + bias_ref[at, :].astype(F32)
                e = jnp.exp(z - jnp.max(z, axis=1, keepdims=True))
                p = e * (1.0 / jnp.sum(e, axis=1, keepdims=True))
                p_ref[at, :] = p
                pb_ref[at, :] = p.astype(BF)

        def attend(b):
            at = pl.ds(b * block, block)
            a = nn(pb_ref[at], v_ref[...]).astype(BF).astype(F32)
            a = jnp.where(own, a, 0.0)
            acc_a[at] += a
            return jnp.sum(u_ref[at].astype(F32) * a, axis=1, keepdims=True)

        def score_grads(b, deltas):
            for i in range(block // step):
                at = pl.ds(b * block + i * step, step)
                ds_ref[at, :] = (
                    p_ref[at, :] * (t_ref[at, :] - deltas[i * step : (i + 1) * step])
                ).astype(BF)
            at = pl.ds(b * block, block)
            acc_q[at] += jnp.where(own, nn(ds_ref[at], k_ref[...]), 0.0)

        scores(0)
        deltas = None
        for b in range(blocks):
            if b + 1 < blocks:
                scores(b + 1)
            slopes(b)
            softmax(b)
            if b > 0:
                score_grads(b - 1, deltas)
            deltas = attend(b)
        score_grads(blocks - 1, deltas)
        dkt[here, :] = nn(qt_ref[here, :], ds_ref[...])
        dvt[here, :] = nn(ut_ref[here, :], pb_ref[...])
        return carry

    lax.fori_loop(0, HEADS, head, 0, unroll=2)
    dq = (acc_q[...] * scale).astype(BF)
    dk = (dkt[...] * scale).astype(BF)
    dv = dvt[...].astype(BF)
    c_ref[...] = (nn(wk_ref[...], dk) + nn(wv_ref[...], dv)).T.astype(BF)
    own_rows = pl.ds(first, rows)
    back = nt(dq, wq_ref[...])
    c_ref[own_rows, :] = (c_ref[own_rows, :].astype(F32) + back).astype(BF)
    weights = (
        tn(xq, dq),
        nn(dk, x).T,
        nn(dv, x).T,
        tn(acc_a[...].astype(BF), gb_ref[...]),
    )
    for i, g in enumerate(weights):
        g_ref[2 * i] = g[:, 0:half]
        g_ref[2 * i + 1] = g[:, half:width]


FAR8 = (4, 3, 5, 2, 6, 1, 7)


def greet(diagonal):
    me = lax.axis_index("space")
    t = lax.axis_index("tm")
    y = lax.rem(me, NY)
    j = lax.rem(t, NJ)
    across = lax.rem(t + NJ, NT)
    far = range(1, NS // NY)
    peers = [{"space": me - y + lax.rem(y + k, NY)} for k in range(1, NY)]
    peers += [{"space": lax.rem(me + NY * k, NS)} for k in far]
    peers += [{"tm": t - j + lax.rem(j + k, NJ)} for k in range(1, NJ)]
    peers.append({"tm": across})
    if diagonal:
        peers += [{"tm": across, "space": lax.rem(me + NY * k, NS)} for k in far]
    barrier = pltpu.get_barrier_semaphore()
    for peer in peers:
        pl.semaphore_signal(barrier, inc=1, device_id=peer, device_id_type=MESH)
    return lambda: pl.semaphore_wait(barrier, len(peers))


def push(src, dst, sems, i, **to):
    return pltpu.make_async_remote_copy(
        src_ref=src,
        dst_ref=dst,
        send_sem=sems[0].at[i],
        recv_sem=sems[1].at[i],
        device_id=to,
        device_id_type=MESH,
    )


def gather_kernel(
    rows, x_in, mask_ref, ct_ref, decay_ref, x_out, b_out, gb_out, grads_ref,
    b_in, got, late, late_in, gb_send, carried, run, prod, before,
    s0, r0, s1, r1, s2, r2, s3, r3, s4, r4, s5, r5, s6, r6, s7, r7, s8, r8, s9, r9, own,
):
    rounds, pad, _ = ct_ref.shape
    cols = b_in.shape[1] // 2
    me = lax.axis_index("space")
    y = lax.rem(me, NY)
    base = me - y
    depth = NS // NY
    z = lax.div(me, NY)
    right, left = lax.rem(z + 1, depth), lax.rem(z + depth - 1, depth)
    t = lax.axis_index("tm")
    core = lax.rem(t, 2)
    j = lax.rem(t, NJ)
    upper = t >= NJ
    half = pl.ds(pl.multiple_of(core * cols, cols), cols)
    all_here = greet(False)
    level = ct_ref[rounds - 1]
    reach = decay_ref[rounds - 1 : rounds, :]
    for r in range(rounds - 2, -1, -1):
        level = ct_ref[r] + decay_ref[r + 1 : r + 2, :] * level
        reach = reach * decay_ref[r : r + 1, :]
    got[j, 0:pad, :] = (decay_ref[0:1, :] * level).astype(BF)
    d0 = reach.astype(BF).astype(F32)
    d1 = (reach - d0).astype(BF).astype(F32)
    d2 = reach - d0 - d1
    row = lax.broadcasted_iota(jnp.int32, (16, reach.shape[1]), 0)
    got[j, pad : pad + 16, :] = jnp.where(row == 0, d0, jnp.where(row == 1, d1, d2)).astype(BF)

    b_in[...] = jnp.full(b_in.shape, NEG, BF)
    bias = jnp.where(mask_ref[...] > 0, 0.0, NEG).astype(F32)
    for group in range(NS):
        b_in[0:rows, group * pad : group * pad + rows] = bias[
            :, group * rows : (group + 1) * rows
        ].astype(BF)

    all_here()
    scan = []
    for k in FAR8:
        to = t - j + lax.rem(j + k, NJ)
        scan.append(push(got.at[j], got.at[j], (s3, r3), k, tm=to))
    tokens = []
    for k in range(1, NY):
        to = lax.rem(y + k, NY)
        tokens.append(push(x_in.at[to], x_out.at[me], (s0, r0), k, space=base + to))
    sides = []
    for k in range(NY):
        slot = base + lax.rem(y - k + NY, NY)
        src = x_in.at[y] if k == 0 else x_out.at[slot]
        sides.append(
            (
                push(src, x_out.at[slot], (s6, r6), k, space=right * NY + y),
                push(src, x_out.at[slot], (s7, r7), k, space=left * NY + y),
            )
        )
    passed = []
    for k in range(NY):
        of, to, sems = (left, right, (s8, r8)) if k < 2 else (right, left, (s9, r9))
        slot = x_out.at[of * NY + lax.rem(y - k + NY, NY)]
        passed.append(push(slot, slot, sems, k, space=to * NY + y))
    masks = []
    for k in range(1, NY):
        to = base + lax.rem(y + k, NY)
        masks.append(push(b_in.at[:, half], b_out.at[y, :, half], (s2, r2), k, space=to))
    local = [
        pltpu.make_async_copy(x_in.at[y], x_out.at[me], own.at[0]),
        pltpu.make_async_copy(b_in, b_out.at[y], own.at[1]),
    ]
    for copy in list(sides[0]) + tokens + scan + masks + local:
        copy.start()
    for k in range(1, NY):
        tokens[k - 1].wait()
        sides[k][0].start()
        sides[k][1].start()

    for copy in scan:
        copy.wait()
    run[...] = jnp.zeros(run.shape, F32)
    prod[...] = jnp.ones(prod.shape, F32)
    for i in range(NJ - 1, -1, -1):

        @pl.when(j == i)
        def _():
            carried[...] = run[...]
            before[...] = prod[...]

        tail = got[i, pad : pad + 16, :].astype(F32)
        step = tail[0:1] + tail[1:2] + tail[2:3]
        run[...] = got[i, 0:pad, :].astype(F32) + step * run[...]
        prod[...] = step * prod[...]
    late[...] = run[...].astype(BF)
    over = push(late, late_in, (s4, r4), 0, tm=lax.rem(t + NJ, NT))
    pl.when(upper)(over.start)
    for k in range(3):
        sides[k][0 if k < 2 else 1].wait()
        passed[k].start()

    @pl.when(jnp.logical_not(upper))
    def _():
        over.wait_recv()
        carried[...] += before[0:1, :] * late_in[...].astype(F32)

    level = ct_ref[rounds - 1] + carried[...]
    for r in range(rounds - 1, -1, -1):
        if r < rounds - 1:
            level = ct_ref[r] + decay_ref[r + 1 : r + 2, :] * level
        grads_ref[r] = level
        gb_send[r] = level.astype(BF)
    ups = []
    for k in range(1, NY):
        to = lax.rem(y + k, NY)
        ups.append(push(gb_send.at[to], gb_out.at[y], (s1, r1), k, space=base + to))
    ups.append(pltpu.make_async_copy(gb_send.at[y], gb_out.at[y], own.at[2]))
    for copy in ups:
        copy.start()

    sides[3][1].wait()
    passed[3].start()
    shared = []
    for k in range(1, NY):
        masks[k - 1].wait()
        piece = b_out.at[lax.rem(y - k + NY, NY), :, half]
        copy = push(piece, piece, (s5, r5), k, tm=t + 1 - 2 * core)
        copy.start()
        shared.append(copy)
    pl.when(upper)(over.wait_send)
    for copy in (sides[0][1], sides[1][1], sides[2][0], sides[3][0]):
        copy.wait()
    for copy in passed + local + ups + shared:
        copy.wait()


def scatter_kernel(
    c_in, g_in, c_out, g_out, send1, got1, part, send2, got2, send3, got3, got4,
    far_l, far_r, mix_l, mix_r, got_l, got_r, sum_c, s0, r0, s1, r1, s2, r2, s3, r3, s4, r4, s5, r5, s6, r6,
):
    me = lax.axis_index("space")
    t = lax.axis_index("tm")
    y = lax.rem(me, NY)
    base = me - y
    j = lax.rem(t, NJ)
    z = lax.div(me, NY)
    depth = NS // NY
    right, left, opposite = (lax.rem(z + k, depth) for k in (1, depth - 1, 2))
    line = z * 2 + lax.div(t, NJ)
    all_here = greet(True)
    for i in range(NJ):
        send1[i] = g_in[i].astype(send1.dtype)
    all_here()

    first = []
    for k in FAR8:
        to = lax.rem(j + k, NJ)
        first.append(push(send1.at[to], got1.at[j], (s0, r0), k, tm=t - j + to))
    two = 2
    far = [
        push(c_in.at[pl.ds(opposite * NY, two)], far_l, (s4, r4), 0, space=right * NY + y),
        push(c_in.at[pl.ds(opposite * NY + two, two)], far_r, (s4, r4), 1, space=left * NY + y),
    ]
    near = [
        push(
            c_in.at[pl.ds(right * NY + two, two)], got_l.at[pl.ds(two, two)], (s4, r4), 2,
            space=right * NY + y,
        ),
        push(
            c_in.at[pl.ds(left * NY, two)], got_r.at[pl.ds(0, two)], (s4, r4), 3,
            space=left * NY + y,
        ),
    ]
    for copy in far + first + near:
        copy.start()
    mixed = [
        push(mix_r, got_l.at[pl.ds(0, two)], (s4, r4), 4, space=right * NY + y),
        push(mix_l, got_r.at[pl.ds(two, two)], (s4, r4), 5, space=left * NY + y),
    ]
    total = g_in[j]
    for copy in first:
        copy.wait()
    for k in range(1, NJ):
        total = total + got1[lax.rem(j + k, NJ)].astype(F32)
    part[...] = total.reshape(part.shape)
    send2[...] = part[...].astype(send2.dtype)

    second = []
    for k in range(1, NY):
        to = lax.rem(y + k, NY)
        second.append(push(send2.at[to], got2.at[y], (s1, r1), k, space=base + to))
    for copy in second:
        copy.start()
    far[0].wait()
    for i in range(two):
        mix_r[i] = (c_in[right * NY + i].astype(F32) + far_l[i].astype(F32)).astype(BF)
    mixed[0].start()
    far[1].wait()
    for i in range(two):
        mix_l[i] = (c_in[left * NY + two + i].astype(F32) + far_r[i].astype(F32)).astype(BF)
    mixed[1].start()
    total = part[y]
    for copy in second:
        copy.wait()
    for k in range(1, NY):
        total = total + got2[lax.rem(y + k, NY)].astype(F32)
    send3[...] = total.astype(send3.dtype)
    got3[line] = send3[...]

    third = []
    for k in FAR8:
        to = lax.rem(line + k, NZ)
        third.append(
            push(
                send3, got3.at[line], (s2, r2), k,
                tm=lax.rem(to, 2) * NJ + j, space=lax.div(to, 2) * NY + y,
            )
        )
    for copy in third:
        copy.start()
    for copy in third:
        copy.wait()
    total = got3[0].astype(F32)
    for i in range(1, NZ):
        total = total + got3[i].astype(F32)
    got4[y] = total.astype(got4.dtype)

    fourth = []
    for k in range(1, NY):
        to = base + lax.rem(y + k, NY)
        fourth.append(push(got4.at[y], got4.at[y], (s3, r3), k, space=to))
    for copy in fourth:
        copy.start()
    for copy in fourth:
        copy.wait()
    g_out[j] = got4[...].reshape(g_out.shape[1:])

    fifth = []
    for k in FAR8:
        to = t - j + lax.rem(j + k, NJ)
        fifth.append(push(g_out.at[j], g_out.at[j], (s5, r5), k, tm=to))
    for copy in fifth:
        copy.start()
    for copy in near + mixed:
        copy.wait()
    for i in range(NY):
        block = c_in[z * NY + i].astype(F32) + got_l[i].astype(F32) + got_r[i].astype(F32)
        sum_c[i] = block.astype(BF)
    tokens = []
    for k in range(1, NY):
        to = lax.rem(y + k, NY)
        tokens.append(push(sum_c.at[to], c_out.at[y], (s6, r6), k, space=base + to))
    for copy in tokens:
        copy.start()
    c_out[y] = sum_c[y]
    for copy in fifth + tokens:
        copy.wait()


def dma(n):
    return pltpu.SemaphoreType.DMA((n,))


def shards(tokens, w_query, w_key, w_value, w_out, mask, decay, cotangent):
    rows, rounds, width = tokens.shape
    pad = -(-rows // 16) * 16
    keys = NS * pad
    quads = NY * pad
    size = width // HEADS
    scale = 1.0 / math.sqrt(size)

    widen = ((0, 0), (0, pad - rows), (0, 0))
    x = jnp.pad(jnp.swapaxes(tokens, 0, 1), widen)
    ct = jnp.pad(jnp.swapaxes(cotangent, 0, 1), widen)

    x_all, bias_all, gb_all, grads = pl.pallas_call(
        functools.partial(gather_kernel, rows),
        out_shape=(
            sds((NS, pad, width), BF),
            sds((NY, pad, keys), BF),
            sds((NY, pad, width), BF),
            sds((rounds, pad, width), F32),
        ),
        in_specs=[ANY, VM, VM, VM],
        out_specs=[ANY, ANY, ANY, VM],
        scratch_shapes=[
            pltpu.VMEM((pad, keys), BF),
            pltpu.VMEM((NJ, pad + 16, width), BF),
            pltpu.VMEM((pad, width), BF),
            pltpu.VMEM((pad, width), BF),
            pltpu.VMEM((rounds, pad, width), BF),
            pltpu.VMEM((pad, width), F32),
            pltpu.VMEM((pad, width), F32),
            pltpu.VMEM((8, width), F32),
            pltpu.VMEM((8, width), F32),
            dma(NY), dma(NY), dma(NY), dma(NY), dma(NY), dma(NY),
            dma(NJ), dma(NJ), dma(1), dma(1), dma(NY), dma(NY),
            dma(NY), dma(NY), dma(NY), dma(NY), dma(NY), dma(NY), dma(NY), dma(NY), dma(3),
        ],
        compiler_params=params(cid=1),
        name="gather",
    )(x, mask, ct, decay)

    c, g = pl.pallas_call(
        functools.partial(attention_kernel, scale),
        out_shape=(sds((keys, width), BF), sds((8, width, width // 2), F32)),
        in_specs=[VM] * 7,
        out_specs=[VM] * 2,
        scratch_shapes=[
            pltpu.VMEM((keys, width), BF),
            pltpu.VMEM((keys, width), BF),
            pltpu.VMEM((width, keys), BF),
            pltpu.VMEM((width, keys), BF),
            pltpu.VMEM((width, quads), BF),
            pltpu.VMEM((quads, width), BF),
            pltpu.VMEM((width, quads), BF),
            pltpu.VMEM((HEADS, quads, size), BF),
            pltpu.VMEM((HEADS, quads, size), BF),
            pltpu.VMEM((quads, keys), F32),
            pltpu.VMEM((quads, keys), F32),
            pltpu.VMEM((quads, keys), BF),
            pltpu.VMEM((quads, keys), F32),
            pltpu.VMEM((quads, keys), BF),
            pltpu.VMEM((quads, width), F32),
            pltpu.VMEM((quads, width), F32),
            pltpu.VMEM((width, keys), F32),
            pltpu.VMEM((width, keys), F32),
        ],
        compiler_params=params(42),
        name="attention",
    )(
        x_all.reshape(keys, width),
        gb_all.reshape(quads, width),
        bias_all.reshape(quads, keys),
        w_query, w_key, w_value, w_out,
    )

    wire = BF
    parts, g = pl.pallas_call(
        scatter_kernel,
        out_shape=(sds((rounds, pad, width), BF), sds((NJ, 256, 128), wire)),
        in_specs=[VM, VM],
        out_specs=[VM, VM],
        scratch_shapes=[
            pltpu.VMEM((NJ, 256, 128), wire),
            pltpu.VMEM((NJ, 256, 128), wire),
            pltpu.VMEM((NY, 64, 128), F32),
            pltpu.VMEM((NY, 64, 128), wire),
            pltpu.VMEM((NY, 64, 128), wire),
            pltpu.VMEM((64, 128), wire),
            pltpu.VMEM((NZ, 64, 128), wire),
            pltpu.VMEM((NY, 64, 128), wire),
            pltpu.VMEM((2, pad, width), BF),
            pltpu.VMEM((2, pad, width), BF),
            pltpu.VMEM((2, pad, width), BF),
            pltpu.VMEM((2, pad, width), BF),
            pltpu.VMEM((NY, pad, width), BF),
            pltpu.VMEM((NY, pad, width), BF),
            pltpu.VMEM((NY, pad, width), BF),
            dma(NJ), dma(NJ), dma(NY), dma(NY), dma(NZ), dma(NZ), dma(NY), dma(NY),
            dma(6), dma(6), dma(NJ), dma(NJ), dma(NY), dma(NY),
        ],
        compiler_params=params(cid=2),
        name="scatter",
    )(c.reshape(NS, pad, width), g)
    gt = grads + parts.astype(F32)
    g = g.astype(F32).reshape(4, 2, width, 128)
    g = jnp.concatenate([g[:, 0], g[:, 1]], axis=2)
    grad_tokens = jnp.swapaxes(gt[:, :rows], 0, 1)
    return (grad_tokens, g[0], g[1], g[2], g[3])


def solution(mesh):
    return jax.shard_map(
        shards,
        mesh=mesh,
        in_specs=(
            P("space", "tm", None),
            P(),
            P(),
            P(),
            P(),
            P("space", None),
            P("tm", None),
            P("space", "tm", None),
        ),
        out_specs=(P("space", "tm", None), P(), P(), P(), P()),
        check_vma=False,
    )
```

```python
import functools
import math

import jax
import jax.numpy as jnp
from jax import lax
from jax.experimental import pallas as pl
from jax.experimental.pallas import tpu as pltpu
from jax.sharding import PartitionSpec as P

HEADS = 8
NS = 16
NT = 16
NY = 4
NJ = 8
NZ = 8
MESH = pl.DeviceIdType.MESH
BF = jnp.bfloat16
F32 = jnp.float32
NEG = -1e30
MIB = 1 << 20

VM = pl.BlockSpec(memory_space=pltpu.VMEM)
ANY = pl.BlockSpec(memory_space=pl.ANY)


def params(mib=16, cid=None):
    if cid is None:
        return pltpu.CompilerParams(vmem_limit_bytes=mib * MIB)
    return pltpu.CompilerParams(
        vmem_limit_bytes=mib * MIB, collective_id=cid, has_side_effects=True
    )


def sds(shape, dtype):
    return jax.ShapeDtypeStruct(shape, dtype)


def nt(a, b):
    return lax.dot_general(a, b, (((1,), (1,)), ((), ())), preferred_element_type=F32)


def tn(a, b):
    return lax.dot_general(a, b, (((0,), (0,)), ((), ())), preferred_element_type=F32)


def nn(a, b):
    return jnp.dot(a, b, preferred_element_type=F32)


def attention_kernel(
    scale, x_ref, gb_ref, bias_ref, wq_ref, wk_ref, wv_ref, wo_ref, c_ref, g_ref,
    k_ref, v_ref, kt_ref, vt_ref, qt_ref, u_ref, ut_ref, q32, u32,
    s_ref, p_ref, pb_ref, t_ref, ds_ref, acc_q, acc_a, dkt, dvt,
):
    rows, width = gb_ref.shape
    size = width // HEADS
    half = width // 2
    first = pl.multiple_of(lax.axis_index("space") // NY * rows, rows)
    x = x_ref[...]
    xq = x_ref[pl.ds(first, rows), :]
    k_ref[...] = nn(x, wk_ref[...]).astype(BF)
    v_ref[...] = nn(x, wv_ref[...]).astype(BF)
    kt_ref[...] = nt(wk_ref[...].T, x).astype(BF)
    vt_ref[...] = nt(wv_ref[...].T, x).astype(BF)
    q = nn(xq, wq_ref[...]).astype(BF)
    qt_ref[...] = nt(wq_ref[...].T, xq).astype(BF)
    u_ref[...] = nt(gb_ref[...], wo_ref[...]).astype(BF)
    ut_ref[...] = nt(wo_ref[...], gb_ref[...]).astype(BF)
    for h in range(HEADS):
        q32[h] = q[:, h * size : (h + 1) * size]
        u32[h] = u_ref[:, h * size : (h + 1) * size]
    acc_q[...] = jnp.zeros_like(acc_q)
    acc_a[...] = jnp.zeros_like(acc_a)
    block, step = rows // 2, 16
    blocks = rows // block

    def head(h, carry):
        here = pl.ds(pl.multiple_of(h * size, size), size)
        own = lax.broadcasted_iota(jnp.int32, (block, width), 1) // size == h

        def scores(b):
            at = pl.ds(b * block, block)
            s_ref[at] = nn(q32[h, at, :], kt_ref[here, :])

        def slopes(b):
            at = pl.ds(b * block, block)
            t_ref[at] = nn(u32[h, at, :], vt_ref[here, :])

        def softmax(b):
            for i in range(block // step):
                at = pl.ds(b * block + i * step, step)
                z = s_ref[at, :] * scale + bias_ref[at, :].astype(F32)
                e = jnp.exp(z - jnp.max(z, axis=1, keepdims=True))
                p = e * (1.0 / jnp.sum(e, axis=1, keepdims=True))
                p_ref[at, :] = p
                pb_ref[at, :] = p.astype(BF)

        def attend(b):
            at = pl.ds(b * block, block)
            a = nn(pb_ref[at], v_ref[...]).astype(BF).astype(F32)
            a = jnp.where(own, a, 0.0)
            acc_a[at] += a
            return jnp.sum(u_ref[at].astype(F32) * a, axis=1, keepdims=True)

        def score_grads(b, deltas):
            for i in range(block // step):
                at = pl.ds(b * block + i * step, step)
                ds_ref[at, :] = (
                    p_ref[at, :] * (t_ref[at, :] - deltas[i * step : (i + 1) * step])
                ).astype(BF)
            at = pl.ds(b * block, block)
            acc_q[at] += jnp.where(own, nn(ds_ref[at], k_ref[...]), 0.0)

        scores(0)
        deltas = None
        for b in range(blocks):
            if b + 1 < blocks:
                scores(b + 1)
            slopes(b)
            softmax(b)
            if b > 0:
                score_grads(b - 1, deltas)
            deltas = attend(b)
        score_grads(blocks - 1, deltas)
        dkt[here, :] = nn(qt_ref[here, :], ds_ref[...])
        dvt[here, :] = nn(ut_ref[here, :], pb_ref[...])
        return carry

    lax.fori_loop(0, HEADS, head, 0, unroll=4)
    dq = (acc_q[...] * scale).astype(BF)
    dk = (dkt[...] * scale).astype(BF)
    dv = dvt[...].astype(BF)
    c_ref[...] = (nn(wk_ref[...], dk) + nn(wv_ref[...], dv)).T.astype(BF)
    own_rows = pl.ds(first, rows)
    back = nt(dq, wq_ref[...])
    c_ref[own_rows, :] = (c_ref[own_rows, :].astype(F32) + back).astype(BF)
    weights = (
        tn(xq, dq),
        nn(dk, x).T,
        nn(dv, x).T,
        tn(acc_a[...].astype(BF), gb_ref[...]),
    )
    for i, g in enumerate(weights):
        g_ref[2 * i] = g[:, 0:half]
        g_ref[2 * i + 1] = g[:, half:width]


FAR8 = (4, 3, 5, 2, 6, 1, 7)


def greet(diagonal):
    me = lax.axis_index("space")
    t = lax.axis_index("tm")
    y = lax.rem(me, NY)
    j = lax.rem(t, NJ)
    across = lax.rem(t + NJ, NT)
    far = range(1, NS // NY)
    peers = [{"space": me - y + lax.rem(y + k, NY)} for k in range(1, NY)]
    peers += [{"space": lax.rem(me + NY * k, NS)} for k in far]
    peers += [{"tm": t - j + lax.rem(j + k, NJ)} for k in range(1, NJ)]
    peers.append({"tm": across})
    if diagonal:
        peers += [{"tm": across, "space": lax.rem(me + NY * k, NS)} for k in far]
    barrier = pltpu.get_barrier_semaphore()
    for peer in peers:
        pl.semaphore_signal(barrier, inc=1, device_id=peer, device_id_type=MESH)
    return lambda: pl.semaphore_wait(barrier, len(peers))


def push(src, dst, sems, i, **to):
    return pltpu.make_async_remote_copy(
        src_ref=src,
        dst_ref=dst,
        send_sem=sems[0].at[i],
        recv_sem=sems[1].at[i],
        device_id=to,
        device_id_type=MESH,
    )


def gather_kernel(
    rows, x_in, mask_ref, ct_ref, decay_ref, x_out, b_out, gb_out, grads_ref,
    b_in, got, late, late_in, gb_send, carried, run, prod, before,
    s0, r0, s1, r1, s2, r2, s3, r3, s4, r4, s5, r5, s6, r6, s7, r7, s8, r8, s9, r9, own,
):
    rounds, pad, _ = ct_ref.shape
    cols = b_in.shape[1] // 2
    me = lax.axis_index("space")
    y = lax.rem(me, NY)
    base = me - y
    depth = NS // NY
    z = lax.div(me, NY)
    right, left = lax.rem(z + 1, depth), lax.rem(z + depth - 1, depth)
    t = lax.axis_index("tm")
    core = lax.rem(t, 2)
    j = lax.rem(t, NJ)
    upper = t >= NJ
    half = pl.ds(pl.multiple_of(core * cols, cols), cols)
    all_here = greet(False)
    level = ct_ref[rounds - 1]
    reach = decay_ref[rounds - 1 : rounds, :]
    for r in range(rounds - 2, -1, -1):
        level = ct_ref[r] + decay_ref[r + 1 : r + 2, :] * level
        reach = reach * decay_ref[r : r + 1, :]
    got[j, 0:pad, :] = (decay_ref[0:1, :] * level).astype(BF)
    d0 = reach.astype(BF).astype(F32)
    d1 = (reach - d0).astype(BF).astype(F32)
    d2 = reach - d0 - d1
    row = lax.broadcasted_iota(jnp.int32, (16, reach.shape[1]), 0)
    got[j, pad : pad + 16, :] = jnp.where(row == 0, d0, jnp.where(row == 1, d1, d2)).astype(BF)

    b_in[...] = jnp.full(b_in.shape, NEG, BF)
    bias = jnp.where(mask_ref[...] > 0, 0.0, NEG).astype(F32)
    for group in range(NS):
        b_in[0:rows, group * pad : group * pad + rows] = bias[
            :, group * rows : (group + 1) * rows
        ].astype(BF)

    all_here()
    scan = []
    for k in FAR8:
        to = t - j + lax.rem(j + k, NJ)
        scan.append(push(got.at[j], got.at[j], (s3, r3), k, tm=to))
    tokens = []
    for k in range(1, NY):
        to = lax.rem(y + k, NY)
        tokens.append(push(x_in.at[to], x_out.at[me], (s0, r0), k, space=base + to))
    sides = []
    for k in range(NY):
        slot = base + lax.rem(y - k + NY, NY)
        src = x_in.at[y] if k == 0 else x_out.at[slot]
        sides.append(
            (
                push(src, x_out.at[slot], (s6, r6), k, space=right * NY + y),
                push(src, x_out.at[slot], (s7, r7), k, space=left * NY + y),
            )
        )
    passed = []
    for k in range(NY):
        of, to, sems = (left, right, (s8, r8)) if k < 2 else (right, left, (s9, r9))
        slot = x_out.at[of * NY + lax.rem(y - k + NY, NY)]
        passed.append(push(slot, slot, sems, k, space=to * NY + y))
    masks = []
    for k in range(1, NY):
        to = base + lax.rem(y + k, NY)
        masks.append(push(b_in.at[:, half], b_out.at[y, :, half], (s2, r2), k, space=to))
    local = [
        pltpu.make_async_copy(x_in.at[y], x_out.at[me], own.at[0]),
        pltpu.make_async_copy(b_in, b_out.at[y], own.at[1]),
    ]
    for copy in list(sides[0]) + tokens + scan + masks + local:
        copy.start()
    for k in range(1, NY):
        tokens[k - 1].wait()
        sides[k][0].start()
        sides[k][1].start()

    for copy in scan:
        copy.wait()
    run[...] = jnp.zeros(run.shape, F32)
    prod[...] = jnp.ones(prod.shape, F32)
    for i in range(NJ - 1, -1, -1):

        @pl.when(j == i)
        def _():
            carried[...] = run[...]
            before[...] = prod[...]

        tail = got[i, pad : pad + 16, :].astype(F32)
        step = tail[0:1] + tail[1:2] + tail[2:3]
        run[...] = got[i, 0:pad, :].astype(F32) + step * run[...]
        prod[...] = step * prod[...]
    late[...] = run[...].astype(BF)
    over = push(late, late_in, (s4, r4), 0, tm=lax.rem(t + NJ, NT))
    pl.when(upper)(over.start)
    for k in range(3):
        sides[k][0 if k < 2 else 1].wait()
        passed[k].start()

    @pl.when(jnp.logical_not(upper))
    def _():
        over.wait_recv()
        carried[...] += before[0:1, :] * late_in[...].astype(F32)

    level = ct_ref[rounds - 1] + carried[...]
    for r in range(rounds - 1, -1, -1):
        if r < rounds - 1:
            level = ct_ref[r] + decay_ref[r + 1 : r + 2, :] * level
        grads_ref[r] = level
        gb_send[r] = level.astype(BF)
    ups = []
    for k in range(1, NY):
        to = lax.rem(y + k, NY)
        ups.append(push(gb_send.at[to], gb_out.at[y], (s1, r1), k, space=base + to))
    ups.append(pltpu.make_async_copy(gb_send.at[y], gb_out.at[y], own.at[2]))
    for copy in ups:
        copy.start()

    sides[3][1].wait()
    passed[3].start()
    shared = []
    for k in range(1, NY):
        masks[k - 1].wait()
        piece = b_out.at[lax.rem(y - k + NY, NY), :, half]
        copy = push(piece, piece, (s5, r5), k, tm=t + 1 - 2 * core)
        copy.start()
        shared.append(copy)
    pl.when(upper)(over.wait_send)
    for copy in (sides[0][1], sides[1][1], sides[2][0], sides[3][0]):
        copy.wait()
    for copy in passed + local + ups + shared:
        copy.wait()


def scatter_kernel(
    c_in, g_in, c_out, g_out, send1, got1, part, send2, got2, send3, got3, got4,
    far_l, far_r, mix_l, mix_r, got_l, got_r, sum_c, s0, r0, s1, r1, s2, r2, s3, r3, s4, r4, s5, r5, s6, r6,
):
    me = lax.axis_index("space")
    t = lax.axis_index("tm")
    y = lax.rem(me, NY)
    base = me - y
    j = lax.rem(t, NJ)
    z = lax.div(me, NY)
    depth = NS // NY
    right, left, opposite = (lax.rem(z + k, depth) for k in (1, depth - 1, 2))
    line = z * 2 + lax.div(t, NJ)
    all_here = greet(True)
    for i in range(NJ):
        send1[i] = g_in[i].astype(send1.dtype)
    all_here()

    first = []
    for k in FAR8:
        to = lax.rem(j + k, NJ)
        first.append(push(send1.at[to], got1.at[j], (s0, r0), k, tm=t - j + to))
    two = 2
    far = [
        push(c_in.at[pl.ds(opposite * NY, two)], far_l, (s4, r4), 0, space=right * NY + y),
        push(c_in.at[pl.ds(opposite * NY + two, two)], far_r, (s4, r4), 1, space=left * NY + y),
    ]
    near = [
        push(
            c_in.at[pl.ds(right * NY + two, two)], got_l.at[pl.ds(two, two)], (s4, r4), 2,
            space=right * NY + y,
        ),
        push(
            c_in.at[pl.ds(left * NY, two)], got_r.at[pl.ds(0, two)], (s4, r4), 3,
            space=left * NY + y,
        ),
    ]
    for copy in far + first + near:
        copy.start()
    mixed = [
        push(mix_r, got_l.at[pl.ds(0, two)], (s4, r4), 4, space=right * NY + y),
        push(mix_l, got_r.at[pl.ds(two, two)], (s4, r4), 5, space=left * NY + y),
    ]
    total = g_in[j]
    for copy in first:
        copy.wait()
    for k in range(1, NJ):
        total = total + got1[lax.rem(j + k, NJ)].astype(F32)
    part[...] = total.reshape(part.shape)
    send2[...] = part[...].astype(send2.dtype)

    second = []
    for k in (2, 1, 3):
        to = lax.rem(y + k, NY)
        second.append(push(send2.at[to], got2.at[y], (s1, r1), k, space=base + to))
    for copy in second:
        copy.start()
    far[0].wait()
    for i in range(two):
        mix_r[i] = (c_in[right * NY + i].astype(F32) + far_l[i].astype(F32)).astype(BF)
    mixed[0].start()
    far[1].wait()
    for i in range(two):
        mix_l[i] = (c_in[left * NY + two + i].astype(F32) + far_r[i].astype(F32)).astype(BF)
    mixed[1].start()
    total = part[y]
    for copy in second:
        copy.wait()
    for k in range(1, NY):
        total = total + got2[lax.rem(y + k, NY)].astype(F32)
    send3[...] = total.astype(send3.dtype)
    got3[line] = send3[...]

    third = []
    for k in FAR8:
        to = lax.rem(line + k, NZ)
        third.append(
            push(
                send3, got3.at[line], (s2, r2), k,
                tm=lax.rem(to, 2) * NJ + j, space=lax.div(to, 2) * NY + y,
            )
        )
    for copy in third:
        copy.start()
    for copy in third:
        copy.wait()
    total = got3[0].astype(F32)
    for i in range(1, NZ):
        total = total + got3[i].astype(F32)
    got4[y] = total.astype(got4.dtype)

    fourth = []
    for k in (2, 1, 3):
        to = base + lax.rem(y + k, NY)
        fourth.append(push(got4.at[y], got4.at[y], (s3, r3), k, space=to))
    for copy in fourth:
        copy.start()
    for copy in fourth:
        copy.wait()
    g_out[j] = got4[...].reshape(g_out.shape[1:])

    fifth = []
    for k in FAR8:
        to = t - j + lax.rem(j + k, NJ)
        fifth.append(push(g_out.at[j], g_out.at[j], (s5, r5), k, tm=to))
    for copy in fifth:
        copy.start()
    for copy in near + mixed:
        copy.wait()
    for i in range(NY):
        block = c_in[z * NY + i].astype(F32) + got_l[i].astype(F32) + got_r[i].astype(F32)
        sum_c[i] = block.astype(BF)
    tokens = []
    for k in range(1, NY):
        to = lax.rem(y + k, NY)
        tokens.append(push(sum_c.at[to], c_out.at[y], (s6, r6), k, space=base + to))
    for copy in tokens:
        copy.start()
    c_out[y] = sum_c[y]
    for copy in fifth + tokens:
        copy.wait()


def dma(n):
    return pltpu.SemaphoreType.DMA((n,))


def shards(tokens, w_query, w_key, w_value, w_out, mask, decay, cotangent):
    rows, rounds, width = tokens.shape
    pad = -(-rows // 16) * 16
    keys = NS * pad
    quads = NY * pad
    size = width // HEADS
    scale = 1.0 / math.sqrt(size)

    widen = ((0, 0), (0, pad - rows), (0, 0))
    x = jnp.pad(jnp.swapaxes(tokens, 0, 1), widen)
    ct = jnp.pad(jnp.swapaxes(cotangent, 0, 1), widen)

    x_all, bias_all, gb_all, grads = pl.pallas_call(
        functools.partial(gather_kernel, rows),
        out_shape=(
            sds((NS, pad, width), BF),
            sds((NY, pad, keys), BF),
            sds((NY, pad, width), BF),
            sds((rounds, pad, width), F32),
        ),
        in_specs=[ANY, VM, VM, VM],
        out_specs=[ANY, ANY, ANY, VM],
        scratch_shapes=[
            pltpu.VMEM((pad, keys), BF),
            pltpu.VMEM((NJ, pad + 16, width), BF),
            pltpu.VMEM((pad, width), BF),
            pltpu.VMEM((pad, width), BF),
            pltpu.VMEM((rounds, pad, width), BF),
            pltpu.VMEM((pad, width), F32),
            pltpu.VMEM((pad, width), F32),
            pltpu.VMEM((8, width), F32),
            pltpu.VMEM((8, width), F32),
            dma(NY), dma(NY), dma(NY), dma(NY), dma(NY), dma(NY),
            dma(NJ), dma(NJ), dma(1), dma(1), dma(NY), dma(NY),
            dma(NY), dma(NY), dma(NY), dma(NY), dma(NY), dma(NY), dma(NY), dma(NY), dma(3),
        ],
        compiler_params=params(cid=1),
        name="gather",
    )(x, mask, ct, decay)

    c, g = pl.pallas_call(
        functools.partial(attention_kernel, scale),
        out_shape=(sds((keys, width), BF), sds((8, width, width // 2), F32)),
        in_specs=[VM] * 7,
        out_specs=[VM] * 2,
        scratch_shapes=[
            pltpu.VMEM((keys, width), BF),
            pltpu.VMEM((keys, width), BF),
            pltpu.VMEM((width, keys), BF),
            pltpu.VMEM((width, keys), BF),
            pltpu.VMEM((width, quads), BF),
            pltpu.VMEM((quads, width), BF),
            pltpu.VMEM((width, quads), BF),
            pltpu.VMEM((HEADS, quads, size), BF),
            pltpu.VMEM((HEADS, quads, size), BF),
            pltpu.VMEM((quads, keys), F32),
            pltpu.VMEM((quads, keys), F32),
            pltpu.VMEM((quads, keys), BF),
            pltpu.VMEM((quads, keys), F32),
            pltpu.VMEM((quads, keys), BF),
            pltpu.VMEM((quads, width), F32),
            pltpu.VMEM((quads, width), F32),
            pltpu.VMEM((width, keys), F32),
            pltpu.VMEM((width, keys), F32),
        ],
        compiler_params=params(42),
        name="attention",
    )(
        x_all.reshape(keys, width),
        gb_all.reshape(quads, width),
        bias_all.reshape(quads, keys),
        w_query, w_key, w_value, w_out,
    )

    wire = BF
    parts, g = pl.pallas_call(
        scatter_kernel,
        out_shape=(sds((rounds, pad, width), BF), sds((NJ, 256, 128), wire)),
        in_specs=[VM, VM],
        out_specs=[VM, VM],
        scratch_shapes=[
            pltpu.VMEM((NJ, 256, 128), wire),
            pltpu.VMEM((NJ, 256, 128), wire),
            pltpu.VMEM((NY, 64, 128), F32),
            pltpu.VMEM((NY, 64, 128), wire),
            pltpu.VMEM((NY, 64, 128), wire),
            pltpu.VMEM((64, 128), wire),
            pltpu.VMEM((NZ, 64, 128), wire),
            pltpu.VMEM((NY, 64, 128), wire),
            pltpu.VMEM((2, pad, width), BF),
            pltpu.VMEM((2, pad, width), BF),
            pltpu.VMEM((2, pad, width), BF),
            pltpu.VMEM((2, pad, width), BF),
            pltpu.VMEM((NY, pad, width), BF),
            pltpu.VMEM((NY, pad, width), BF),
            pltpu.VMEM((NY, pad, width), BF),
            dma(NJ), dma(NJ), dma(NY), dma(NY), dma(NZ), dma(NZ), dma(NY), dma(NY),
            dma(6), dma(6), dma(NJ), dma(NJ), dma(NY), dma(NY),
        ],
        compiler_params=params(cid=2),
        name="scatter",
    )(c.reshape(NS, pad, width), g)
    gt = grads + parts.astype(F32)
    g = g.astype(F32).reshape(4, 2, width, 128)
    g = jnp.concatenate([g[:, 0], g[:, 1]], axis=2)
    grad_tokens = jnp.swapaxes(gt[:, :rows], 0, 1)
    return (grad_tokens, g[0], g[1], g[2], g[3])


def solution(mesh):
    return jax.shard_map(
        shards,
        mesh=mesh,
        in_specs=(
            P("space", "tm", None),
            P(),
            P(),
            P(),
            P(),
            P("space", None),
            P("tm", None),
            P("space", "tm", None),
        ),
        out_specs=(P("space", "tm", None), P(), P(), P(), P()),
        check_vma=False,
    )
```
